768 devices in a mesh: seq: 32 (over x, y), head: 24 (over z, core).
Axes of the slice: x: 4, y: 8, z: 12, core: 2. Of those that a mesh axis runs over, the one named last changes fastest.
Arguments:
- queries: bfloat16 [16384, 3072], P('seq', 'head'), may hold values from -6 to 6
- key_rows: bfloat16 [16384, 3072], P('seq', 'head'), may hold values from -6 to 6
- value_rows: bfloat16 [16384, 3072], P('seq', 'head'), may hold values from -6 to 6
- upstream: bfloat16 [16384, 3072], P('seq', 'head'), may hold values from -6 to 6
- exit_weight: bfloat16 [3072], P('head'), may hold values from -4 to 4
- labels: int32 [16384], P('seq'), may hold values 0 or 1
- rand_blocks: int32 [256, 3], replicated, may hold values from 0 to 255, as said below
- glob_blocks: int32 [2], replicated, may hold values from 0 to 255, as said below
Outputs:
- attended: bfloat16 [16384, 3072], P('seq', 'head')
- token_loss: float32 [16384], P('seq')
- grad_query: float32 [16384, 3072], P('seq', 'head')
- grad_key: float32 [16384, 3072], P('seq', 'head')
- grad_value: float32 [16384, 3072], P('seq', 'head')
The draws below stay inside these ranges and needn't reach their ends.
Inputs may be any that keep to these rules, and one draw needn't show every extreme that they name: `rand_blocks`: among the 24 entries of the rows of one device (aligned groups of 8 rows), at most 1 lie in any one aligned range of 8 key blocks, and some range holds exactly 1. `glob_blocks`: 2 distinct blocks, the same for every query block; the document's last block is always among them.
All inputs are finite; a program needn't handle non-finite values. No bound on the sum of `labels` on one device may be relied on, other than what follows from the above.
Results may differ from the reference program's by a relative error of at most 0.018.
Values may be sent and summed in bfloat16 or wider, within the bound.
No kernel may reach another device: no remote copies, remote signals or barrier semaphores. Data moves between devices by JAX's collectives and lax.ppermute only.
A program may use at most 64 MiB of HBM per device.

```python
import math
import jax
import jax.numpy as jnp
from jax import lax

HEAD_SIZE = 128
BLOCK = 64
RAND = 3
GLOBAL = 2
BPD = 8
HEADS = 24
SLOTS = 8
DOC_TOKENS = 16384
NBLOCKS = 256
RAND_DEV = 24
CAP_R = 1


def qk_pair(key):
    columns = HEADS * HEAD_SIZE
    queries = jnp.clip(jax.random.normal(jax.random.fold_in(key, 21), (DOC_TOKENS, columns), jnp.float32), -6.0, 6.0)
    key_vals = jnp.clip(jax.random.normal(jax.random.fold_in(key, 22), (DOC_TOKENS, columns), jnp.float32), -6.0, 6.0)
    return (queries, key_vals)


def draw_queries(key, part):
    return qk_pair(key)[0].astype(jnp.bfloat16)


def draw_key_rows(key, part):
    return qk_pair(key)[1].astype(jnp.bfloat16)


def draw_exit_weight(key, part):
    columns = HEADS * HEAD_SIZE
    ramp = (jnp.arange(columns) // HEAD_SIZE).astype(jnp.float32) / max(HEADS - 1, 1)
    values = 0.2 * (1.0 + 2.0 * ramp) * jnp.clip(jax.random.normal(jax.random.fold_in(key, 32), (columns,), jnp.float32), -6.0, 6.0)
    return values.astype(jnp.bfloat16)


def draw_rand_blocks(key, part):
    shards = NBLOCKS // BPD
    busy_owner = jax.random.randint(jax.random.fold_in(key, 7), (), 0, shards)

    def device_draw(device):
        dev_key = jax.random.fold_in(key, 1000 + device)
        spread = jax.random.permutation(jax.random.fold_in(dev_key, 1), (shards - 1) * CAP_R)[:RAND_DEV - CAP_R]
        others = (busy_owner + 1 + spread // CAP_R) % shards
        owners = jnp.concatenate([jnp.zeros((CAP_R,), jnp.int32) + busy_owner, others.astype(jnp.int32)])
        owners = owners[jax.random.permutation(jax.random.fold_in(dev_key, 2), RAND_DEV)]
        offsets = jax.random.randint(jax.random.fold_in(dev_key, 3), (RAND_DEV,), 0, BPD)
        return (owners * BPD + offsets).astype(jnp.int32).reshape(BPD, RAND)
    return jax.vmap(device_draw)(jnp.arange(shards)).reshape(NBLOCKS, RAND).astype(jnp.int32)


def draw_glob_blocks(key, part):
    others = jax.random.permutation(jax.random.fold_in(key, 5), NBLOCKS - 1)[:GLOBAL - 1].astype(jnp.int32)
    chosen = jnp.concatenate([others, jnp.zeros((1,), jnp.int32) + (NBLOCKS - 1)])
    order = jax.random.permutation(jax.random.fold_in(key, 6), GLOBAL)
    return chosen[order].astype(jnp.int32)


def place_ends(values, own_key, smallest, high):
    index_at = [jax.random.randint(jax.random.fold_in(own_key, axis), (), 0, length) for axis, length in enumerate(values.shape)]
    main_axis = values.shape.index(max(values.shape))
    neighbour = index_at[:main_axis] + [(index_at[main_axis] + 1) % values.shape[main_axis]] + index_at[main_axis + 1:]
    return values.at[tuple(index_at)].set(smallest).at[tuple(neighbour)].set(high)


def shard_levels(own_key, extent, cuts, least, high):
    gain = 1.0
    for position, parts in cuts:
        steps = jax.random.uniform(jax.random.fold_in(jax.random.fold_in(own_key, 6), position), (parts,), jnp.float32, least / len(cuts), high / len(cuts))
        gain = gain * jnp.repeat(jnp.exp(steps), extent[position] // parts).reshape((-1,) + (1,) * (len(extent) - 1 - position))
    return gain


def normal_values(own_key, shape, deviation, reach, cuts=(), kind=jnp.bfloat16):
    entries = deviation * jax.random.normal(own_key, shape, jnp.float32)
    if cuts:
        entries = entries * shard_levels(own_key, shape, cuts, -0.22, 0.18)
    return jnp.clip(entries, -reach, reach).astype(kind)


def setup_inputs(seed: int = 0) -> dict:
    arg_keys = jax.random.split(jax.random.key(seed), 9)
    return {
        "queries": draw_queries(jax.random.fold_in(arg_keys[8], 71), 0),
        "key_rows": draw_key_rows(jax.random.fold_in(arg_keys[8], 71), 0),
        "value_rows": normal_values(arg_keys[2], (DOC_TOKENS, HEADS * HEAD_SIZE), 1.0, 6.0, ((0, 32), (1, 24))),
        "upstream": normal_values(arg_keys[3], (DOC_TOKENS, HEADS * HEAD_SIZE), 1.0, 6.0, ((0, 32), (1, 24))),
        "exit_weight": draw_exit_weight(jax.random.fold_in(arg_keys[8], 71), 0),
        "labels": place_ends((jax.random.randint(arg_keys[5], (DOC_TOKENS,), 0, 2) < 1).astype(jnp.int32), jax.random.fold_in(arg_keys[5], 1), 0, 1),
        "rand_blocks": draw_rand_blocks(jax.random.fold_in(arg_keys[8], 71), 0),
        "glob_blocks": draw_glob_blocks(jax.random.fold_in(arg_keys[8], 71), 0),
    }


def build_keys(kv_blocks, rand_blocks, glob_blocks):
    prev_blocks = jnp.roll(kv_blocks, 1, axis=0)
    next_blocks = jnp.roll(kv_blocks, -1, axis=0)
    random_part = kv_blocks[rand_blocks]
    global_part = jnp.broadcast_to(kv_blocks[glob_blocks][None], (NBLOCKS, GLOBAL, BLOCK, 2 * HEAD_SIZE))
    gathered_keys = jnp.concatenate([prev_blocks[:, None], kv_blocks[:, None], next_blocks[:, None], random_part, global_part], axis=1)
    return gathered_keys.reshape(NBLOCKS, SLOTS * BLOCK, 2 * HEAD_SIZE)

def key_valid():
    block_ids = jnp.arange(NBLOCKS)
    slot_ok = jnp.concatenate([(block_ids > 0)[:, None], jnp.ones((NBLOCKS, 1), bool), (block_ids < NBLOCKS - 1)[:, None], jnp.ones((NBLOCKS, RAND + GLOBAL), bool)], axis=1)
    return jnp.repeat(slot_ok, BLOCK, axis=1)

def attention_probs(head_q, gathered_keys):
    blocked_queries = head_q.reshape(NBLOCKS, BLOCK, HEAD_SIZE).astype(jnp.float32)
    attention_scores = jnp.einsum('afs,ans->afn', blocked_queries, gathered_keys[..., :HEAD_SIZE].astype(jnp.float32)) / math.sqrt(HEAD_SIZE)
    attention_scores = jnp.where(key_valid()[:, None, :], attention_scores, -jnp.inf)
    row_peak = lax.optimization_barrier(jnp.max(attention_scores, axis=-1, keepdims=True))
    exp_terms = jnp.exp(attention_scores - row_peak)
    return exp_terms / lax.optimization_barrier(jnp.sum(exp_terms, axis=-1, keepdims=True))

def round_low(values):
    return lax.optimization_barrier(values.astype(jnp.bfloat16)).astype(jnp.float32)

def reference(queries, key_rows, value_rows, upstream, exit_weight, labels, rand_blocks, glob_blocks):

    def split_heads(values):
        return values.reshape(DOC_TOKENS, HEADS, HEAD_SIZE).transpose(1, 0, 2)
    q_heads = split_heads(queries)
    kv_heads = jnp.concatenate([split_heads(key_rows), split_heads(value_rows)], axis=-1)

    def forward_one(inputs):
        head_q, head_kv = inputs
        gathered_keys = build_keys(head_kv.reshape(NBLOCKS, BLOCK, 2 * HEAD_SIZE), rand_blocks, glob_blocks)
        reduced_probabilities = attention_probs(head_q, gathered_keys).astype(jnp.bfloat16)
        head_output = jnp.einsum('omc,och->omh', reduced_probabilities.astype(jnp.float32), gathered_keys[..., HEAD_SIZE:].astype(jnp.float32))
        return head_output.astype(jnp.bfloat16).reshape(DOC_TOKENS, HEAD_SIZE)
    heads_out = lax.map(forward_one, (q_heads, kv_heads))
    attended = heads_out.transpose(1, 0, 2).reshape(DOC_TOKENS, HEADS * HEAD_SIZE)
    logits = jnp.dot(attended, exit_weight, preferred_element_type=jnp.float32)
    target = labels.astype(jnp.float32)
    token_loss = jax.nn.softplus(logits) - target * logits
    dlogits = jax.nn.sigmoid(logits) - target
    grad_out = (upstream.astype(jnp.float32) + dlogits[:, None] * exit_weight.astype(jnp.float32)[None, :]).astype(jnp.bfloat16)
    g_heads = split_heads(grad_out)

    def backward_one(inputs):
        head_q, head_kv, head_g = inputs
        gathered_keys = build_keys(head_kv.reshape(NBLOCKS, BLOCK, 2 * HEAD_SIZE), rand_blocks, glob_blocks)
        probs = attention_probs(head_q, gathered_keys)
        reduced_probabilities = probs.astype(jnp.bfloat16).astype(jnp.float32)
        key_portion = gathered_keys[..., :HEAD_SIZE].astype(jnp.float32)
        value_portion = gathered_keys[..., HEAD_SIZE:].astype(jnp.float32)
        block_gradient = head_g.reshape(NBLOCKS, BLOCK, HEAD_SIZE).astype(jnp.float32)
        blocked_queries = head_q.reshape(NBLOCKS, BLOCK, HEAD_SIZE).astype(jnp.float32)
        probability_gradient = jnp.einsum('afs,ans->afn', block_gradient, value_portion)
        row_dot = lax.optimization_barrier(jnp.sum(probs * probability_gradient, axis=-1, keepdims=True))
        score_gradient = (probs * (probability_gradient - row_dot) / math.sqrt(HEAD_SIZE)).astype(jnp.bfloat16).astype(jnp.float32)
        head_query_gradient = jnp.einsum('omc,och->omh', score_gradient, key_portion).reshape(DOC_TOKENS, HEAD_SIZE)
        key_gradient = jnp.einsum('tnc,tny->tcy', score_gradient, blocked_queries)
        value_gradient = jnp.einsum('tnc,tny->tcy', reduced_probabilities, block_gradient)
        slot_grads = jnp.concatenate([key_gradient, value_gradient], axis=-1).reshape(NBLOCKS, SLOTS, BLOCK, 2 * HEAD_SIZE)
        to_prev = round_low(slot_grads[:, 0])
        to_next = round_low(slot_grads[:, 2])
        rand_grads = round_low(slot_grads[:, 3:3 + RAND])
        zero_block = jnp.zeros((1, BLOCK, 2 * HEAD_SIZE), jnp.float32)
        kv_total = slot_grads[:, 1] + jnp.concatenate([to_prev[1:], zero_block], axis=0) + jnp.concatenate([zero_block, to_next[:-1]], axis=0)
        kv_total = kv_total.at[rand_blocks.reshape(-1)].add(rand_grads.reshape(NBLOCKS * RAND, BLOCK, 2 * HEAD_SIZE))
        kv_total = kv_total.at[glob_blocks].add(lax.optimization_barrier(jnp.sum(slot_grads[:, 3 + RAND:], axis=0)))
        return (head_query_gradient, kv_total.reshape(DOC_TOKENS, 2 * HEAD_SIZE))
    dq_heads, dkv_heads = lax.map(backward_one, (q_heads, kv_heads, g_heads))
    grad_query = dq_heads.transpose(1, 0, 2).reshape(DOC_TOKENS, HEADS * HEAD_SIZE)
    grad_key = dkv_heads[..., :HEAD_SIZE].transpose(1, 0, 2).reshape(DOC_TOKENS, HEADS * HEAD_SIZE)
    grad_value = dkv_heads[..., HEAD_SIZE:].transpose(1, 0, 2).reshape(DOC_TOKENS, HEADS * HEAD_SIZE)
    return (attended, token_loss, grad_query, grad_key, grad_value)
```

```python
import math

import jax
import jax.numpy as jnp
from jax import lax
from jax.experimental import pallas as pl
from jax.experimental.pallas import tpu as pltpu
from jax.sharding import PartitionSpec as P

BLOCK = 64
RAND = 3
GLOBAL = 2
CHUNK = 8

NT = (((1,), (1,)), ((), ()))
NN = (((1,), (0,)), ((), ()))
TN = (((0,), (0,)), ((), ()))


def mm(a, b, dims):
    return lax.dot_general(a, b, dims, preferred_element_type=jnp.float32)


def smem(count):
    return [pl.BlockSpec(memory_space=pltpu.SMEM) for _ in range(count)]


def vmem(count):
    return [pl.BlockSpec(memory_space=pltpu.VMEM) for _ in range(count)]


def call(kernel, name, n_smem, n_vmem, outs, **kw):
    return pl.pallas_call(
        kernel,
        name=name,
        in_specs=smem(n_smem) + vmem(n_vmem),
        out_specs=tuple(vmem(len(outs))),
        out_shape=tuple(jax.ShapeDtypeStruct(s, d) for s, d in outs),
        compiler_params=pltpu.CompilerParams(vmem_limit_bytes=40 * 1024 * 1024),
        **kw,
    )


def pack_kernel(pick, glob, k, v, send, gsend, first, last):
    blocks = k.shape[0]
    shards = send.shape[0]
    for r in range(shards):
        at = jnp.maximum(pick[r], 0)
        send[r, :BLOCK] = k[at]
        send[r, BLOCK:] = v[at]
    per_block = 2 * BLOCK // CHUNK
    for g in range(GLOBAL):
        at = glob[g] % blocks
        kg = k[at]
        vg = v[at]
        for c in range(per_block):
            src = kg if c < per_block // 2 else vg
            lo = (c * CHUNK) % BLOCK
            gsend[g * per_block + c] = src[lo : lo + CHUNK]
    first[:BLOCK] = k[0]
    first[BLOCK:] = v[0]
    last[:BLOCK] = k[blocks - 1]
    last[BLOCK:] = v[blocks - 1]


def slots_of(i, base, local, prev, after, incoming, shared, rand, blocks):
    parts = [
        local[i - 1] if i > 0 else prev[base : base + BLOCK],
        local[i],
        local[i + 1] if i < blocks - 1 else after[base : base + BLOCK],
    ]
    for j in range(RAND):
        parts.append(incoming[rand[i, j] // blocks, base : base + BLOCK])
    for g in range(GLOBAL):
        lo = g * 2 * BLOCK + base
        parts.append(shared[lo : lo + BLOCK])
    return jnp.concatenate(parts, axis=0)


def forward_kernel(rand, me, q, k, v, prev, after, incoming, shared, weight, attended, probs, part):
    blocks = k.shape[0]
    head_dim = k.shape[2]
    keys = (3 + RAND + GLOBAL) * BLOCK
    inv_sqrt = 1.0 / math.sqrt(head_dim)
    w8 = jnp.broadcast_to(weight[...], (8, head_dim))
    lane = lax.broadcasted_iota(jnp.int32, (BLOCK, keys), 1)
    rows = []
    for i in range(blocks):
        kk = slots_of(i, 0, k, prev, after, incoming, shared, rand, blocks)
        vv = slots_of(i, BLOCK, v, prev, after, incoming, shared, rand, blocks)
        s = mm(q[i], kk, NT) * inv_sqrt
        if i == 0:
            s = jnp.where((lane < BLOCK) & (me[0] == 0), -jnp.inf, s)
        if i == blocks - 1:
            void = (lane >= 2 * BLOCK) & (lane < 3 * BLOCK)
            s = jnp.where(void & (me[0] == me[1] - 1), -jnp.inf, s)
        e = jnp.exp(s - jnp.max(s, axis=1, keepdims=True))
        p = e / jnp.sum(e, axis=1, keepdims=True)
        probs[i] = p
        a = mm(p.astype(jnp.bfloat16), vv, NN).astype(jnp.bfloat16)
        attended[i] = a
        rows.append(mm(w8, a, NT)[:1])
    row = jnp.concatenate(rows, axis=1)
    for r in range(part.shape[0]):
        part[r] = row


def backward_kernel(
    rand, me, parts, labels, q, k, v, prev, after, incoming, shared, weight, upstream, probs,
    grad_q, acc_k, acc_v, outgoing, gparts, to_prev, to_next,
):
    blocks = k.shape[0]
    head_dim = k.shape[2]
    inv_sqrt = 1.0 / math.sqrt(head_dim)
    bf16 = jnp.bfloat16
    logits = jnp.sum(parts[...], axis=0)
    slope = lax.logistic(logits) - labels[...].astype(jnp.float32)
    column = jnp.transpose(jnp.broadcast_to(slope, (8, slope.shape[1])))[:, :1]
    w = weight[...].astype(jnp.float32)
    glob = [jnp.zeros((BLOCK, head_dim), jnp.float32) for _ in range(2 * GLOBAL)]
    own = []
    for i in range(blocks):
        kk = slots_of(i, 0, k, prev, after, incoming, shared, rand, blocks)
        vv = slots_of(i, BLOCK, v, prev, after, incoming, shared, rand, blocks)
        p = probs[i]
        g = (upstream[i].astype(jnp.float32) + column[i * BLOCK : (i + 1) * BLOCK] * w).astype(bf16)
        dp = mm(g, vv, NT)
        dot = jnp.sum(p * dp, axis=1, keepdims=True)
        ds = (p * (dp - dot) * inv_sqrt).astype(bf16)
        grad_q[i] = mm(ds, kk, NN)
        dk = mm(ds, q[i], TN)
        dv = mm(p.astype(bf16), g, TN)
        for j in range(RAND):
            lo = (3 + j) * BLOCK
            at = rand[i, j] // blocks
            outgoing[at, :BLOCK] = dk[lo : lo + BLOCK].astype(bf16)
            outgoing[at, BLOCK:] = dv[lo : lo + BLOCK].astype(bf16)
        for n in range(GLOBAL):
            lo = (3 + RAND + n) * BLOCK
            glob[2 * n] = glob[2 * n] + dk[lo : lo + BLOCK]
            glob[2 * n + 1] = glob[2 * n + 1] + dv[lo : lo + BLOCK]
        own.append((dk[: 3 * BLOCK], dv[: 3 * BLOCK]))
    for which, acc in enumerate((acc_k, acc_v)):
        lo = which * BLOCK
        for i in range(blocks):
            total = own[i][which][BLOCK : 2 * BLOCK]
            if i < blocks - 1:
                total = total + own[i + 1][which][:BLOCK].astype(bf16).astype(jnp.float32)
            if i > 0:
                total = total + own[i - 1][which][2 * BLOCK :].astype(bf16).astype(jnp.float32)
            acc[i] = total
        to_prev[lo : lo + BLOCK] = own[0][which][:BLOCK].astype(bf16)
        to_next[lo : lo + BLOCK] = own[blocks - 1][which][2 * BLOCK :].astype(bf16)
    for n in range(2 * GLOBAL):
        gparts[n * BLOCK : (n + 1) * BLOCK] = glob[n].astype(bf16)


def final_kernel(pick, glob, me, acc_k, acc_v, back, from_prev, from_next, shared, out_k, out_v):
    blocks = acc_k.shape[0]
    shards = back.shape[0]
    f32 = jnp.float32
    out_k[...] = acc_k[...]
    out_v[...] = acc_v[...]
    out_k[0] = out_k[0] + from_prev[:BLOCK].astype(f32)
    out_v[0] = out_v[0] + from_prev[BLOCK:].astype(f32)
    out_k[blocks - 1] = out_k[blocks - 1] + from_next[:BLOCK].astype(f32)
    out_v[blocks - 1] = out_v[blocks - 1] + from_next[BLOCK:].astype(f32)
    for r in range(shards):
        at = pick[r]

        @pl.when(at >= 0)
        def _():
            out_k[at] = out_k[at] + back[r, :BLOCK].astype(f32)
            out_v[at] = out_v[at] + back[r, BLOCK:].astype(f32)

    for g in range(GLOBAL):

        @pl.when(glob[g] // blocks == me[0])
        def _():
            at = glob[g] % blocks
            lo = g * 2 * BLOCK
            out_k[at] = out_k[at] + shared[lo : lo + BLOCK].astype(f32)
            out_v[at] = out_v[at] + shared[lo + BLOCK : lo + 2 * BLOCK].astype(f32)


def exchange(x, axis):
    return lax.all_to_all(x, axis, split_axis=0, concat_axis=0, tiled=True)


def body(queries, key_rows, value_rows, upstream, exit_weight, labels, rand_blocks, glob_blocks):
    tokens, head_dim = queries.shape
    blocks = tokens // BLOCK
    shards = lax.axis_size("seq")
    heads = lax.axis_size("head")
    myself = lax.axis_index("seq")
    bf16 = jnp.bfloat16
    f32 = jnp.float32
    keys = (3 + RAND + GLOBAL) * BLOCK
    wide = 2 * BLOCK
    chunks = GLOBAL * wide // CHUNK
    ups = [(n, n + 1) for n in range(shards - 1)]
    downs = [(n + 1, n) for n in range(shards - 1)]

    me = jnp.stack([myself, jnp.full_like(myself, shards)]).astype(jnp.int32)
    rand = lax.dynamic_slice_in_dim(rand_blocks, myself * blocks, blocks, 0)
    mine = jnp.where(rand_blocks // blocks == myself, rand_blocks % blocks, -1)
    pick = jnp.max(jnp.max(mine, axis=1).reshape(shards, blocks), axis=1)

    q = queries.reshape(blocks, BLOCK, head_dim)
    k = key_rows.reshape(blocks, BLOCK, head_dim)
    v = value_rows.reshape(blocks, BLOCK, head_dim)
    up = upstream.reshape(blocks, BLOCK, head_dim)
    weight = exit_weight.reshape(1, head_dim)

    send, gsend, first, last = call(
        pack_kernel, "pack", 2, 2,
        [((shards, wide, head_dim), bf16), ((chunks, CHUNK, head_dim), bf16),
         ((wide, head_dim), bf16), ((wide, head_dim), bf16)],
    )(pick, glob_blocks, k, v)
    incoming = exchange(send, "seq")
    glob_got = exchange(gsend, "seq")
    prev = lax.ppermute(last, "seq", ups)
    after = lax.ppermute(first, "seq", downs)
    owner = glob_blocks[myself // (shards // GLOBAL)] // blocks
    piece = lax.dynamic_index_in_dim(glob_got, owner, 0, keepdims=True)
    shared = exchange(jnp.broadcast_to(piece, (shards, CHUNK, head_dim)), "seq")
    shared = shared.reshape(GLOBAL * wide, head_dim)

    attended, probs, part = call(
        forward_kernel, "forward", 2, 8,
        [((blocks, BLOCK, head_dim), bf16), ((blocks, BLOCK, keys), f32), ((heads, 1, tokens), f32)],
    )(rand, me, q, k, v, prev, after, incoming, shared, weight)
    parts = exchange(part, "head")

    acc3 = (blocks, BLOCK, head_dim)
    grad_q, acc_k, acc_v, outgoing, gparts, to_prev, to_next = call(
        backward_kernel, "backward", 2, 12,
        [(acc3, f32), (acc3, f32), (acc3, f32), ((shards, wide, head_dim), bf16),
         ((GLOBAL * wide, head_dim), bf16), ((wide, head_dim), bf16), ((wide, head_dim), bf16)],
    )(rand, me, parts, labels.reshape(1, tokens), q, k, v, prev, after, incoming, shared, weight, up, probs)
    back = exchange(outgoing, "seq")
    gback = exchange(gparts.reshape(chunks, CHUNK, head_dim), "seq")
    from_prev = lax.ppermute(to_next, "seq", ups)
    from_next = lax.ppermute(to_prev, "seq", downs)
    gsum = jnp.sum(gback.astype(f32), axis=0, keepdims=True).astype(bf16)
    gtotal = exchange(jnp.broadcast_to(gsum, (shards, CHUNK, head_dim)), "seq")
    gtotal = gtotal.reshape(GLOBAL * wide, head_dim)

    logits = jnp.sum(parts, axis=(0, 1))
    token_loss = jax.nn.softplus(logits) - labels.astype(f32) * logits

    out_k, out_v = call(
        final_kernel, "final", 3, 6, [(acc3, f32), (acc3, f32)],
        input_output_aliases={3: 0, 4: 1},
    )(pick, glob_blocks, me, acc_k, acc_v, back, from_prev, from_next, gtotal)
    flat = (tokens, head_dim)
    return (
        attended.reshape(flat),
        token_loss,
        grad_q.reshape(flat),
        out_k.reshape(flat),
        out_v.reshape(flat),
    )


def solution(mesh):
    placed = (
        P("seq", "head"),
        P("seq", "head"),
        P("seq", "head"),
        P("seq", "head"),
        P("head"),
        P("seq"),
        P(),
        P(),
    )
    return jax.shard_map(
        body,
        mesh=mesh,
        in_specs=placed,
        out_specs=(
            P("seq", "head"),
            P("seq"),
            P("seq", "head"),
            P("seq", "head"),
            P("seq", "head"),
        ),
        check_vma=False,
    )
```

```python
import math

import jax
import jax.numpy as jnp
from jax import lax
from jax.experimental import pallas as pl
from jax.experimental.pallas import tpu as pltpu
from jax.sharding import PartitionSpec as P

BLOCK = 64
RAND = 3
GLOBAL = 2
CHUNK = 8

NT = (((1,), (1,)), ((), ()))
NN = (((1,), (0,)), ((), ()))
TN = (((0,), (0,)), ((), ()))


def mm(a, b, dims):
    return lax.dot_general(a, b, dims, preferred_element_type=jnp.float32)


def smem(count):
    return [pl.BlockSpec(memory_space=pltpu.SMEM) for _ in range(count)]


def vmem(count):
    return [pl.BlockSpec(memory_space=pltpu.VMEM) for _ in range(count)]


def call(kernel, name, n_smem, n_vmem, outs, **kw):
    return pl.pallas_call(
        kernel,
        name=name,
        in_specs=smem(n_smem) + vmem(n_vmem),
        out_specs=tuple(vmem(len(outs))),
        out_shape=tuple(jax.ShapeDtypeStruct(s, d) for s, d in outs),
        compiler_params=pltpu.CompilerParams(vmem_limit_bytes=40 * 1024 * 1024),
        **kw,
    )


def scatter_kernel(glob, k, v, gsend, staged, sems):
    blocks = k.shape[0]
    copies = []
    for g in range(GLOBAL):
        at = glob[g] % blocks
        for n, src in enumerate((k, v)):
            slot = 2 * g + n
            copies.append(pltpu.make_async_copy(src.at[at], staged.at[slot], sems.at[slot]))
    for copy in copies:
        copy.start()
    per_block = BLOCK // CHUNK
    for slot, copy in enumerate(copies):
        copy.wait()
        for c in range(per_block):
            gsend[slot * per_block + c] = staged[slot, c * CHUNK : (c + 1) * CHUNK]


def pack_kernel(pick, k, v, weight, labels, send, first, last, weight_out, labels_out):
    blocks = k.shape[0]
    for r in range(send.shape[0]):
        at = jnp.maximum(pick[r], 0)
        send[r, :BLOCK] = k[at]
        send[r, BLOCK : 2 * BLOCK] = v[at]
        send[r, 2 * BLOCK :] = jnp.zeros((CHUNK, k.shape[2]), k.dtype)
    first[:BLOCK] = k[0]
    first[BLOCK:] = v[0]
    last[:BLOCK] = k[blocks - 1]
    last[BLOCK:] = v[blocks - 1]
    weight_out[...] = weight[...].astype(jnp.float32)
    labels_out[...] = labels[...].astype(jnp.float32)


def fill_kernel(glob, me, got, send, out, sems):
    del send
    shards = got.shape[0]
    owner = glob[me[0] // (shards // GLOBAL)] // me[2]
    copies = [
        pltpu.make_async_copy(got.at[owner], out.at[r, 2 * BLOCK :], sems.at[r])
        for r in range(shards)
    ]
    for copy in copies:
        copy.start()
    for copy in copies:
        copy.wait()


def shared_rows(incoming, slot):
    per_block = BLOCK // CHUNK
    lo = slot * per_block
    rows = incoming[lo : lo + per_block, 2 * BLOCK :]
    return rows.reshape(BLOCK, rows.shape[2])


def slots_of(i, base, local, prev, after, incoming, shared, rand, blocks):
    parts = [
        local[i - 1] if i > 0 else prev[base : base + BLOCK],
        local[i],
        local[i + 1] if i < blocks - 1 else after[base : base + BLOCK],
    ]
    for j in range(RAND):
        parts.append(incoming[rand[i, j] // blocks, base : base + BLOCK])
    parts.extend(shared)
    return jnp.concatenate(parts, axis=0)


def forward_kernel(rand, me, q, k, v, prev, after, incoming, weight, attended, probs, part):
    blocks = k.shape[0]
    head_dim = k.shape[2]
    keys = (3 + RAND + GLOBAL) * BLOCK
    inv_sqrt = 1.0 / math.sqrt(head_dim)
    w8 = jnp.broadcast_to(weight[...], (8, head_dim)).astype(jnp.bfloat16)
    gk = [shared_rows(incoming, 2 * g) for g in range(GLOBAL)]
    gv = [shared_rows(incoming, 2 * g + 1) for g in range(GLOBAL)]
    lane = lax.broadcasted_iota(jnp.int32, (BLOCK, keys), 1)
    rows = []
    for i in range(blocks):
        kk = slots_of(i, 0, k, prev, after, incoming, gk, rand, blocks)
        vv = slots_of(i, BLOCK, v, prev, after, incoming, gv, rand, blocks)
        s = mm(q[i], kk, NT) * inv_sqrt
        if i == 0:
            s = jnp.where((lane < BLOCK) & (me[0] == 0), -jnp.inf, s)
        if i == blocks - 1:
            void = (lane >= 2 * BLOCK) & (lane < 3 * BLOCK)
            s = jnp.where(void & (me[0] == me[1] - 1), -jnp.inf, s)
        e = jnp.exp(s - jnp.max(s, axis=1, keepdims=True))
        p = e / jnp.sum(e, axis=1, keepdims=True)
        probs[i] = p
        a = mm(p.astype(jnp.bfloat16), vv, NN).astype(jnp.bfloat16)
        attended[i] = a
        rows.append(mm(w8, a, NT)[:1])
    row = jnp.concatenate(rows, axis=1)
    for r in range(part.shape[0]):
        part[r] = row


def backward_kernel(
    rand, parts, labels, q, k, v, prev, after, incoming, weight, upstream, probs,
    grad_q, acc_k, acc_v, outgoing, to_prev, to_next,
):
    blocks = k.shape[0]
    head_dim = k.shape[2]
    inv_sqrt = 1.0 / math.sqrt(head_dim)
    bf16 = jnp.bfloat16
    logits = jnp.sum(parts[...], axis=0)
    slope = lax.logistic(logits) - labels[...]
    column = jnp.transpose(jnp.broadcast_to(slope, (8, slope.shape[1])))[:, :1]
    w = weight[...]
    gk = [shared_rows(incoming, 2 * g) for g in range(GLOBAL)]
    gv = [shared_rows(incoming, 2 * g + 1) for g in range(GLOBAL)]
    glob = [jnp.zeros((BLOCK, head_dim), jnp.float32) for _ in range(2 * GLOBAL)]
    own = []
    for i in range(blocks):
        kk = slots_of(i, 0, k, prev, after, incoming, gk, rand, blocks)
        vv = slots_of(i, BLOCK, v, prev, after, incoming, gv, rand, blocks)
        p = probs[i]
        g = (upstream[i].astype(jnp.float32) + column[i * BLOCK : (i + 1) * BLOCK] * w).astype(bf16)
        dp = mm(g, vv, NT)
        dot = jnp.sum(p * dp, axis=1, keepdims=True)
        ds = (p * (dp - dot) * inv_sqrt).astype(bf16)
        grad_q[i] = mm(ds, kk, NN)
        dk = mm(ds, q[i], TN)
        dv = mm(p.astype(bf16), g, TN)
        for j in range(RAND):
            lo = (3 + j) * BLOCK
            at = rand[i, j] // blocks
            outgoing[at, :BLOCK] = dk[lo : lo + BLOCK].astype(bf16)
            outgoing[at, BLOCK : 2 * BLOCK] = dv[lo : lo + BLOCK].astype(bf16)
        for n in range(GLOBAL):
            lo = (3 + RAND + n) * BLOCK
            glob[2 * n] = glob[2 * n] + dk[lo : lo + BLOCK]
            glob[2 * n + 1] = glob[2 * n + 1] + dv[lo : lo + BLOCK]
        own.append((dk[: 3 * BLOCK], dv[: 3 * BLOCK]))
    for which, acc in enumerate((acc_k, acc_v)):
        lo = which * BLOCK
        for i in range(blocks):
            total = own[i][which][BLOCK : 2 * BLOCK]
            if i < blocks - 1:
                total = total + own[i + 1][which][:BLOCK].astype(bf16).astype(jnp.float32)
            if i > 0:
                total = total + own[i - 1][which][2 * BLOCK :].astype(bf16).astype(jnp.float32)
            acc[i] = total
        to_prev[lo : lo + BLOCK] = own[0][which][:BLOCK].astype(bf16)
        to_next[lo : lo + BLOCK] = own[blocks - 1][which][2 * BLOCK :].astype(bf16)
    per_block = BLOCK // CHUNK
    for n in range(2 * GLOBAL):
        rows = glob[n].astype(bf16).reshape(per_block, CHUNK, head_dim)
        outgoing[n * per_block : (n + 1) * per_block, 2 * BLOCK :] = rows


def final_kernel(pick, glob, me, acc_k, acc_v, back, from_prev, from_next, shared, out_k, out_v):
    blocks = acc_k.shape[0]
    shards = back.shape[0]
    f32 = jnp.float32
    out_k[...] = acc_k[...]
    out_v[...] = acc_v[...]
    out_k[0] = out_k[0] + from_prev[:BLOCK].astype(f32)
    out_v[0] = out_v[0] + from_prev[BLOCK:].astype(f32)
    out_k[blocks - 1] = out_k[blocks - 1] + from_next[:BLOCK].astype(f32)
    out_v[blocks - 1] = out_v[blocks - 1] + from_next[BLOCK:].astype(f32)
    for r in range(shards):
        at = pick[r]

        @pl.when(at >= 0)
        def _():
            out_k[at] = out_k[at] + back[r, :BLOCK].astype(f32)
            out_v[at] = out_v[at] + back[r, BLOCK : 2 * BLOCK].astype(f32)

    for g in range(GLOBAL):

        @pl.when(glob[g] // blocks == me[0])
        def _():
            at = glob[g] % blocks
            lo = g * 2 * BLOCK
            out_k[at] = out_k[at] + shared[lo : lo + BLOCK].astype(f32)
            out_v[at] = out_v[at] + shared[lo + BLOCK : lo + 2 * BLOCK].astype(f32)


def exchange(x, axis):
    return lax.all_to_all(x, axis, split_axis=0, concat_axis=0, tiled=True)


def body(queries, key_rows, value_rows, upstream, exit_weight, labels, rand_blocks, glob_blocks):
    tokens, head_dim = queries.shape
    blocks = tokens // BLOCK
    shards = lax.axis_size("seq")
    heads = lax.axis_size("head")
    myself = lax.axis_index("seq")
    bf16 = jnp.bfloat16
    f32 = jnp.float32
    keys = (3 + RAND + GLOBAL) * BLOCK
    wide = 2 * BLOCK
    chunks = GLOBAL * wide // CHUNK
    ups = [(n, n + 1) for n in range(shards - 1)]
    downs = [(n + 1, n) for n in range(shards - 1)]

    me = jnp.stack([myself, jnp.full_like(myself, shards), jnp.full_like(myself, blocks)])
    rand = lax.dynamic_slice_in_dim(rand_blocks, myself * blocks, blocks, 0)
    mine = jnp.where(rand_blocks // blocks == myself, rand_blocks % blocks, -1)
    pick = jnp.max(jnp.max(mine, axis=1).reshape(shards, blocks), axis=1)

    q = queries.reshape(blocks, BLOCK, head_dim)
    k = key_rows.reshape(blocks, BLOCK, head_dim)
    v = value_rows.reshape(blocks, BLOCK, head_dim)
    up = upstream.reshape(blocks, BLOCK, head_dim)
    weight = exit_weight.reshape(1, head_dim)

    slot_rows = wide + CHUNK
    gsend = pl.pallas_call(
        scatter_kernel,
        name="scatter",
        in_specs=smem(1) + [pl.BlockSpec(memory_space=pl.ANY)] * 2,
        out_specs=pl.BlockSpec(memory_space=pltpu.VMEM),
        out_shape=jax.ShapeDtypeStruct((chunks, CHUNK, head_dim), bf16),
        scratch_shapes=[
            pltpu.VMEM((2 * GLOBAL, BLOCK, head_dim), bf16),
            pltpu.SemaphoreType.DMA((2 * GLOBAL,)),
        ],
    )(glob_blocks, k, v)
    glob_got = exchange(gsend, "seq")
    send, first, last, w32, target = call(
        pack_kernel, "pack", 1, 4,
        [((shards, slot_rows, head_dim), bf16), ((wide, head_dim), bf16), ((wide, head_dim), bf16),
         ((1, head_dim), f32), ((1, tokens), f32)],
    )(pick, k, v, weight, labels.reshape(1, tokens))
    prev = lax.ppermute(last, "seq", ups)
    after = lax.ppermute(first, "seq", downs)
    anywhere = pl.BlockSpec(memory_space=pl.ANY)
    send = pl.pallas_call(
        fill_kernel,
        name="fill",
        in_specs=smem(2) + [anywhere] * 2,
        out_specs=anywhere,
        out_shape=jax.ShapeDtypeStruct(send.shape, send.dtype),
        scratch_shapes=[pltpu.SemaphoreType.DMA((shards,))],
        input_output_aliases={3: 0},
    )(glob_blocks, me, glob_got, send)
    incoming = exchange(send, "seq")

    attended, probs, part = call(
        forward_kernel, "forward", 2, 7,
        [((blocks, BLOCK, head_dim), bf16), ((blocks, BLOCK, keys), f32), ((heads, 1, tokens), f32)],
    )(rand, me, q, k, v, prev, after, incoming, w32)
    parts = exchange(part, "head")

    acc3 = (blocks, BLOCK, head_dim)
    grad_q, acc_k, acc_v, outgoing, to_prev, to_next = call(
        backward_kernel, "backward", 1, 11,
        [(acc3, f32), (acc3, f32), (acc3, f32), ((shards, slot_rows, head_dim), bf16),
         ((wide, head_dim), bf16), ((wide, head_dim), bf16)],
    )(rand, parts, target, q, k, v, prev, after, incoming, w32, up, probs)
    back = exchange(outgoing, "seq")
    from_prev = lax.ppermute(to_next, "seq", ups)
    from_next = lax.ppermute(to_prev, "seq", downs)
    gsum = jnp.sum(back[:, wide:].astype(f32), axis=0, keepdims=True).astype(bf16)
    gtotal = exchange(jnp.broadcast_to(gsum, (shards, CHUNK, head_dim)), "seq")
    gtotal = gtotal.reshape(GLOBAL * wide, head_dim)

    logits = jnp.sum(parts, axis=(0, 1))
    token_loss = jax.nn.softplus(logits) - labels.astype(f32) * logits

    out_k, out_v = call(
        final_kernel, "final", 3, 6, [(acc3, f32), (acc3, f32)],
        input_output_aliases={3: 0, 4: 1},
    )(pick, glob_blocks, me, acc_k, acc_v, back, from_prev, from_next, gtotal)
    flat = (tokens, head_dim)
    return (
        attended.reshape(flat),
        token_loss,
        grad_q.reshape(flat),
        out_k.reshape(flat),
        out_v.reshape(flat),
    )


def solution(mesh):
    placed = (
        P("seq", "head"),
        P("seq", "head"),
        P("seq", "head"),
        P("seq", "head"),
        P("head"),
        P("seq"),
        P(),
        P(),
    )
    return jax.shard_map(
        body,
        mesh=mesh,
        in_specs=placed,
        out_specs=(
            P("seq", "head"),
            P("seq"),
            P("seq", "head"),
            P("seq", "head"),
            P("seq", "head"),
        ),
        check_vma=False,
    )
```

```python
import math

import jax
import jax.numpy as jnp
from jax import lax
from jax.experimental import pallas as pl
from jax.experimental.pallas import tpu as pltpu
from jax.sharding import PartitionSpec as P

BLOCK = 64
RAND = 3
GLOBAL = 2
CHUNK = 8

NT = (((1,), (1,)), ((), ()))
NN = (((1,), (0,)), ((), ()))
TN = (((0,), (0,)), ((), ()))


def mm(a, b, dims):
    return lax.dot_general(a, b, dims, preferred_element_type=jnp.float32)


def smem(count):
    return [pl.BlockSpec(memory_space=pltpu.SMEM) for _ in range(count)]


def vmem(count):
    return [pl.BlockSpec(memory_space=pltpu.VMEM) for _ in range(count)]


def params(mib):
    return pltpu.CompilerParams(vmem_limit_bytes=mib * 1024 * 1024)


def call(kernel, name, n_smem, n_vmem, outs, mib, **kw):
    return pl.pallas_call(
        kernel,
        name=name,
        in_specs=smem(n_smem) + vmem(n_vmem),
        out_specs=tuple(vmem(len(outs))),
        out_shape=tuple(jax.ShapeDtypeStruct(s, d) for s, d in outs),
        compiler_params=params(mib),
        **kw,
    )


def scatter_kernel(glob, k, v, out, sems):
    blocks = k.shape[0]
    copies = []
    for g in range(GLOBAL):
        at = glob[g] % blocks
        for n, src in enumerate((k, v)):
            slot = 2 * g + n
            copies.append(pltpu.make_async_copy(src.at[at], out.at[slot], sems.at[slot]))
    for copy in copies:
        copy.start()
    for copy in copies:
        copy.wait()


def pack_kernel(pick, k, v, weight, labels, send, first, last, weight_out, labels_out):
    blocks = k.shape[0]
    for r in range(send.shape[0]):
        at = jnp.maximum(pick[r], 0)
        send[r, :BLOCK] = k[at]
        send[r, BLOCK : 2 * BLOCK] = v[at]
        send[r, 2 * BLOCK :] = jnp.zeros((CHUNK, k.shape[2]), k.dtype)
    first[:BLOCK] = k[0]
    first[BLOCK:] = v[0]
    last[:BLOCK] = k[blocks - 1]
    last[BLOCK:] = v[blocks - 1]
    weight_out[...] = weight[...].astype(jnp.float32)
    labels_out[...] = labels[...].astype(jnp.float32)


def fill_kernel(glob, me, got, send, out, wide, sem):
    del send
    shards = got.shape[0]
    piece = got[glob[me[0] // (shards // GLOBAL)] // me[2]]
    for r in range(shards):
        wide[r] = piece
    copy = pltpu.make_async_copy(wide, out.at[:, 2 * BLOCK :], sem)
    copy.start()
    copy.wait()


def shared_rows(incoming, slot):
    per_block = BLOCK // CHUNK
    lo = slot * per_block
    rows = incoming[lo : lo + per_block, 2 * BLOCK :]
    return rows.reshape(BLOCK, rows.shape[2])


def slots_of(i, base, local, prev, after, incoming, shared, rand, blocks):
    parts = [
        local[i - 1] if i > 0 else prev[base : base + BLOCK],
        local[i],
        local[i + 1] if i < blocks - 1 else after[base : base + BLOCK],
    ]
    for j in range(RAND):
        parts.append(incoming[rand[i, j] // blocks, base : base + BLOCK])
    parts.extend(shared)
    return jnp.concatenate(parts, axis=0)


def forward_kernel(rand, me, q, k, v, prev, after, incoming, weight, attended, probs, part):
    blocks = k.shape[0]
    head_dim = k.shape[2]
    keys = (3 + RAND + GLOBAL) * BLOCK
    inv_sqrt = 1.0 / math.sqrt(head_dim)
    w8 = jnp.broadcast_to(weight[...], (8, head_dim)).astype(jnp.bfloat16)
    gk = [shared_rows(incoming, 2 * g) for g in range(GLOBAL)]
    gv = [shared_rows(incoming, 2 * g + 1) for g in range(GLOBAL)]
    lane = lax.broadcasted_iota(jnp.int32, (BLOCK, keys), 1)
    rows = []
    for i in range(blocks):
        kk = slots_of(i, 0, k, prev, after, incoming, gk, rand, blocks)
        vv = slots_of(i, BLOCK, v, prev, after, incoming, gv, rand, blocks)
        s = mm(q[i], kk, NT) * inv_sqrt
        if i == 0:
            s = jnp.where((lane < BLOCK) & (me[0] == 0), -jnp.inf, s)
        if i == blocks - 1:
            void = (lane >= 2 * BLOCK) & (lane < 3 * BLOCK)
            s = jnp.where(void & (me[0] == me[1] - 1), -jnp.inf, s)
        e = jnp.exp(s - jnp.max(s, axis=1, keepdims=True))
        p = e / jnp.sum(e, axis=1, keepdims=True)
        probs[i] = p
        a = mm(p.astype(jnp.bfloat16), vv, NN).astype(jnp.bfloat16)
        attended[i] = a
        rows.append(mm(w8, a, NT)[:1])
    row = jnp.concatenate(rows, axis=1)
    for r in range(part.shape[0]):
        part[r] = row


def backward_kernel(
    rand, parts, labels, q, k, v, prev, after, incoming, weight, upstream, probs,
    grad_s, grad_o, outgoing, to_prev, to_next,
):
    blocks = k.shape[0]
    head_dim = k.shape[2]
    inv_sqrt = 1.0 / math.sqrt(head_dim)
    bf16 = jnp.bfloat16
    logits = jnp.sum(parts[...], axis=0)
    slope = lax.logistic(logits) - labels[...]
    column = jnp.transpose(jnp.broadcast_to(slope, (8, slope.shape[1])))[:, :1]
    w = weight[...]
    gv = [shared_rows(incoming, 2 * g + 1) for g in range(GLOBAL)]
    far = 3 * BLOCK
    glob = jnp.zeros((GLOBAL * BLOCK, 2 * head_dim), jnp.float32)
    for i in range(blocks):
        vv = slots_of(i, BLOCK, v, prev, after, incoming, gv, rand, blocks)
        p = probs[i]
        g = (upstream[i].astype(jnp.float32) + column[i * BLOCK : (i + 1) * BLOCK] * w).astype(bf16)
        dp = mm(g, vv, NT)
        dot = jnp.sum(p * dp, axis=1, keepdims=True)
        ds = (p * (dp - dot) * inv_sqrt).astype(bf16)
        pb = p.astype(bf16)
        grad_s[i] = ds
        grad_o[i] = g
        dk = mm(ds[:, far:], q[i], TN)
        dv = mm(pb[:, far:], g, TN)
        for j in range(RAND):
            lo = j * BLOCK
            at = rand[i, j] // blocks
            outgoing[at, :BLOCK] = dk[lo : lo + BLOCK].astype(bf16)
            outgoing[at, BLOCK : 2 * BLOCK] = dv[lo : lo + BLOCK].astype(bf16)
        glob = glob + jnp.concatenate([dk[RAND * BLOCK :], dv[RAND * BLOCK :]], axis=1)
        if i == 0:
            to_prev[:BLOCK] = mm(ds[:, :BLOCK], q[i], TN).astype(bf16)
            to_prev[BLOCK:] = mm(pb[:, :BLOCK], g, TN).astype(bf16)
        if i == blocks - 1:
            to_next[:BLOCK] = mm(ds[:, 2 * BLOCK : far], q[i], TN).astype(bf16)
            to_next[BLOCK:] = mm(pb[:, 2 * BLOCK : far], g, TN).astype(bf16)
    per_block = BLOCK // CHUNK
    for n in range(2 * GLOBAL):
        lo = (n // 2) * BLOCK
        col = (n % 2) * head_dim
        rows = glob[lo : lo + BLOCK, col : col + head_dim].astype(bf16)
        outgoing[n * per_block : (n + 1) * per_block, 2 * BLOCK :] = rows.reshape(per_block, CHUNK, head_dim)


def local_kernel(rand, q, k, prev, after, incoming, probs, grad_s, grad_o, grad_q, acc_k, acc_v):
    blocks = k.shape[0]
    bf16 = jnp.bfloat16
    gk = [shared_rows(incoming, 2 * g) for g in range(GLOBAL)]
    own = []
    for i in range(blocks):
        kk = slots_of(i, 0, k, prev, after, incoming, gk, rand, blocks)
        ds = grad_s[i]
        grad_q[i] = mm(ds, kk, NN)
        near = 3 * BLOCK
        dk = mm(ds[:, :near], q[i], TN)
        dv = mm(probs[i, :, :near].astype(bf16), grad_o[i], TN)
        own.append((dk, dv))
    for which, acc in enumerate((acc_k, acc_v)):
        for i in range(blocks):
            total = own[i][which][BLOCK : 2 * BLOCK]
            if i < blocks - 1:
                total = total + own[i + 1][which][:BLOCK].astype(bf16).astype(jnp.float32)
            if i > 0:
                total = total + own[i - 1][which][2 * BLOCK :].astype(bf16).astype(jnp.float32)
            acc[i] = total


def gather_kernel(pick, acc_k, acc_v, back, from_prev, from_next, out_k, out_v):
    blocks = acc_k.shape[0]
    f32 = jnp.float32
    out_k[...] = acc_k[...]
    out_v[...] = acc_v[...]
    out_k[0] = out_k[0] + from_prev[:BLOCK].astype(f32)
    out_v[0] = out_v[0] + from_prev[BLOCK:].astype(f32)
    out_k[blocks - 1] = out_k[blocks - 1] + from_next[:BLOCK].astype(f32)
    out_v[blocks - 1] = out_v[blocks - 1] + from_next[BLOCK:].astype(f32)
    for r in range(back.shape[0]):
        at = pick[r]

        @pl.when(at >= 0)
        def _():
            out_k[at] = out_k[at] + back[r, :BLOCK].astype(f32)
            out_v[at] = out_v[at] + back[r, BLOCK : 2 * BLOCK].astype(f32)


def final_kernel(glob, me, acc_k, acc_v, shared, out_k, out_v):
    blocks = acc_k.shape[0]
    f32 = jnp.float32
    out_k[...] = acc_k[...]
    out_v[...] = acc_v[...]
    for g in range(GLOBAL):

        @pl.when(glob[g] // blocks == me[0])
        def _():
            at = glob[g] % blocks
            lo = g * 2 * BLOCK
            out_k[at] = out_k[at] + shared[lo : lo + BLOCK].astype(f32)
            out_v[at] = out_v[at] + shared[lo + BLOCK : lo + 2 * BLOCK].astype(f32)


def exchange(x, axis):
    return lax.all_to_all(x, axis, split_axis=0, concat_axis=0, tiled=True)


def body(queries, key_rows, value_rows, upstream, exit_weight, labels, rand_blocks, glob_blocks):
    tokens, head_dim = queries.shape
    blocks = tokens // BLOCK
    shards = lax.axis_size("seq")
    heads = lax.axis_size("head")
    myself = lax.axis_index("seq")
    bf16 = jnp.bfloat16
    f32 = jnp.float32
    keys = (3 + RAND + GLOBAL) * BLOCK
    wide = 2 * BLOCK
    chunks = GLOBAL * wide // CHUNK
    ups = [(n, n + 1) for n in range(shards - 1)]
    downs = [(n + 1, n) for n in range(shards - 1)]

    me = jnp.stack([myself, jnp.full_like(myself, shards), jnp.full_like(myself, blocks)])
    rand = lax.dynamic_slice_in_dim(rand_blocks, myself * blocks, blocks, 0)
    mine = jnp.where(rand_blocks // blocks == myself, rand_blocks % blocks, -1)
    pick = jnp.max(jnp.max(mine, axis=1).reshape(shards, blocks), axis=1)

    q = queries.reshape(blocks, BLOCK, head_dim)
    k = key_rows.reshape(blocks, BLOCK, head_dim)
    v = value_rows.reshape(blocks, BLOCK, head_dim)
    up = upstream.reshape(blocks, BLOCK, head_dim)
    weight = exit_weight.reshape(1, head_dim)

    slot_rows = wide + CHUNK
    anywhere = pl.BlockSpec(memory_space=pl.ANY)
    gsend = pl.pallas_call(
        scatter_kernel,
        name="scatter",
        in_specs=smem(1) + [anywhere] * 2,
        out_specs=anywhere,
        out_shape=jax.ShapeDtypeStruct((2 * GLOBAL, BLOCK, head_dim), bf16),
        scratch_shapes=[pltpu.SemaphoreType.DMA((2 * GLOBAL,))],
    )(glob_blocks, k, v).reshape(chunks, CHUNK, head_dim)
    glob_got = exchange(gsend, "seq")
    send, first, last, w32, target = call(
        pack_kernel, "pack", 1, 4,
        [((shards, slot_rows, head_dim), bf16), ((wide, head_dim), bf16), ((wide, head_dim), bf16),
         ((1, head_dim), f32), ((1, tokens), f32)], 6,
    )(pick, k, v, weight, labels.reshape(1, tokens))
    prev = lax.ppermute(last, "seq", ups)
    after = lax.ppermute(first, "seq", downs)
    send = pl.pallas_call(
        fill_kernel,
        name="fill",
        in_specs=smem(2) + vmem(1) + [anywhere],
        out_specs=anywhere,
        out_shape=jax.ShapeDtypeStruct(send.shape, send.dtype),
        scratch_shapes=[pltpu.VMEM((shards, CHUNK, head_dim), bf16), pltpu.SemaphoreType.DMA(())],
        input_output_aliases={3: 0},
        compiler_params=params(2),
    )(glob_blocks, me, glob_got, send)
    incoming = exchange(send, "seq")

    attended, probs, part = call(
        forward_kernel, "forward", 2, 7,
        [((blocks, BLOCK, head_dim), bf16), ((blocks, BLOCK, keys), f32), ((heads, 1, tokens), f32)], 16,
    )(rand, me, q, k, v, prev, after, incoming, w32)
    parts = exchange(part, "head")

    acc3 = (blocks, BLOCK, head_dim)
    grad_s, grad_o, outgoing, to_prev, to_next = call(
        backward_kernel, "backward", 1, 11,
        [((blocks, BLOCK, keys), bf16), (acc3, bf16), ((shards, slot_rows, head_dim), bf16),
         ((wide, head_dim), bf16), ((wide, head_dim), bf16)], 16,
    )(rand, parts, target, q, k, v, prev, after, incoming, w32, up, probs)
    grad_q, acc_k, acc_v = call(local_kernel, "local", 1, 8, [(acc3, f32)] * 3, 16)(
        rand, q, k, prev, after, incoming, probs, grad_s, grad_o
    )
    back = exchange(outgoing, "seq")
    back, acc_k, acc_v = lax.optimization_barrier((back, acc_k, acc_v))
    from_prev = lax.ppermute(to_next, "seq", ups)
    from_next = lax.ppermute(to_prev, "seq", downs)
    gsum = jnp.sum(back[:, wide:].astype(f32), axis=0, keepdims=True).astype(bf16)
    gtotal = exchange(jnp.broadcast_to(gsum, (shards, CHUNK, head_dim)), "seq")
    gtotal = gtotal.reshape(GLOBAL * wide, head_dim)

    logits = jnp.sum(parts, axis=(0, 1))
    token_loss = jax.nn.softplus(logits) - labels.astype(f32) * logits

    acc_k, acc_v = call(gather_kernel, "gather", 1, 5, [(acc3, f32)] * 2, 8)(
        pick, acc_k, acc_v, back, from_prev, from_next
    )
    out_k, out_v = call(final_kernel, "final", 2, 3, [(acc3, f32)] * 2, 6)(
        glob_blocks, me, acc_k, acc_v, gtotal
    )
    flat = (tokens, head_dim)
    return (
        attended.reshape(flat),
        token_loss,
        grad_q.reshape(flat),
        out_k.reshape(flat),
        out_v.reshape(flat),
    )


def solution(mesh):
    placed = (
        P("seq", "head"),
        P("seq", "head"),
        P("seq", "head"),
        P("seq", "head"),
        P("head"),
        P("seq"),
        P(),
        P(),
    )
    return jax.shard_map(
        body,
        mesh=mesh,
        in_specs=placed,
        out_specs=(
            P("seq", "head"),
            P("seq"),
            P("seq", "head"),
            P("seq", "head"),
            P("seq", "head"),
        ),
        check_vma=False,
    )
```

```python
import math

import jax
import jax.numpy as jnp
from jax import lax
from jax.experimental import pallas as pl
from jax.experimental.pallas import tpu as pltpu
from jax.sharding import PartitionSpec as P

BLOCK = 64
RAND = 3
GLOBAL = 2
CHUNK = 8

NT = (((1,), (1,)), ((), ()))
NN = (((1,), (0,)), ((), ()))
TN = (((0,), (0,)), ((), ()))


def mm(a, b, dims):
    return lax.dot_general(a, b, dims, preferred_element_type=jnp.float32)


def smem(count):
    return [pl.BlockSpec(memory_space=pltpu.SMEM) for _ in range(count)]


def vmem(count):
    return [pl.BlockSpec(memory_space=pltpu.VMEM) for _ in range(count)]


def call(kernel, name, n_smem, n_vmem, outs, mib=40, **kw):
    if mib:
        kw["compiler_params"] = pltpu.CompilerParams(vmem_limit_bytes=mib * 1024 * 1024)
    return pl.pallas_call(
        kernel,
        name=name,
        in_specs=smem(n_smem) + vmem(n_vmem),
        out_specs=tuple(vmem(len(outs))),
        out_shape=tuple(jax.ShapeDtypeStruct(s, d) for s, d in outs),
        **kw,
    )


def pack_kernel(pick, glob, k, v, send, first, last):
    blocks = k.shape[0]
    wide = 2 * BLOCK
    per_block = BLOCK // CHUNK
    for r in range(send.shape[0]):
        at = jnp.maximum(pick[r], 0)
        send[r, :BLOCK] = k[at]
        send[r, BLOCK:wide] = v[at]
    for g in range(GLOBAL):
        at = glob[g] % blocks
        for n, src in enumerate((k, v)):
            rows = src[at].reshape(per_block, CHUNK, src.shape[2])
            lo = (2 * g + n) * per_block
            send[lo : lo + per_block, wide:] = rows
    first[:BLOCK] = k[0]
    first[BLOCK:] = v[0]
    last[:BLOCK] = k[blocks - 1]
    last[BLOCK:] = v[blocks - 1]


def near_slots(i, base, local, prev, after, incoming, rand, blocks):
    parts = [
        local[i - 1] if i > 0 else prev[base : base + BLOCK],
        local[i],
        local[i + 1] if i < blocks - 1 else after[base : base + BLOCK],
    ]
    for j in range(RAND):
        parts.append(incoming[rand[i, j] // blocks, base : base + BLOCK])
    return jnp.concatenate(parts, axis=0)


def global_slots(base, shared):
    lows = [g * 2 * BLOCK + base for g in range(GLOBAL)]
    return jnp.concatenate([shared[lo : lo + BLOCK] for lo in lows], axis=0)


def near_kernel(rand, me, q, k, v, prev, after, incoming, terms, out, peak, total):
    blocks = k.shape[0]
    head_dim = k.shape[2]
    keys = (3 + RAND) * BLOCK
    inv_sqrt = 1.0 / math.sqrt(head_dim)
    lane = lax.broadcasted_iota(jnp.int32, (BLOCK, keys), 1)
    for i in range(blocks):
        kk = near_slots(i, 0, k, prev, after, incoming, rand, blocks)
        vv = near_slots(i, BLOCK, v, prev, after, incoming, rand, blocks)
        s = mm(q[i], kk, NT) * inv_sqrt
        if i == 0:
            s = jnp.where((lane < BLOCK) & (me[0] == 0), -jnp.inf, s)
        if i == blocks - 1:
            void = (lane >= 2 * BLOCK) & (lane < 3 * BLOCK)
            s = jnp.where(void & (me[0] == me[1] - 1), -jnp.inf, s)
        m = jnp.max(s, axis=1, keepdims=True)
        e = jnp.exp(s - m)
        terms[i] = e
        out[i] = mm(e.astype(jnp.bfloat16), vv, NN)
        peak[i] = jnp.broadcast_to(m, (BLOCK, head_dim))
        total[i] = jnp.broadcast_to(jnp.sum(e, axis=1, keepdims=True), (BLOCK, head_dim))


def forward_kernel(q, shared, weight, terms, out, peak, total, attended, probs, part):
    blocks = q.shape[0]
    head_dim = q.shape[2]
    near = (3 + RAND) * BLOCK
    inv_sqrt = 1.0 / math.sqrt(head_dim)
    w8 = jnp.broadcast_to(weight[...], (8, head_dim))
    gk = global_slots(0, shared)
    gv = global_slots(BLOCK, shared)
    rows = []
    for i in range(blocks):
        s = mm(q[i], gk, NT) * inv_sqrt
        old = peak[i][:, :1]
        m = jnp.maximum(old, jnp.max(s, axis=1, keepdims=True))
        e = jnp.exp(s - m)
        shift = jnp.exp(old - m)
        inv = 1.0 / (shift * total[i][:, :1] + jnp.sum(e, axis=1, keepdims=True))
        probs[i, :, :near] = terms[i] * (shift * inv)
        probs[i, :, near:] = e * inv
        a = (out[i] * shift + mm(e.astype(jnp.bfloat16), gv, NN)) * inv
        a = a.astype(jnp.bfloat16)
        attended[i] = a
        rows.append(mm(w8, a, NT)[:1])
    row = jnp.concatenate(rows, axis=1)
    for r in range(part.shape[0]):
        part[r] = row


def backward_kernel(
    rand, parts, labels, q, k, v, prev, after, incoming, shared, weight, upstream, probs,
    grad_q, acc_k, acc_v, outgoing, to_prev, to_next,
):
    blocks = k.shape[0]
    head_dim = k.shape[2]
    inv_sqrt = 1.0 / math.sqrt(head_dim)
    bf16 = jnp.bfloat16
    logits = jnp.sum(parts[...], axis=0)
    slope = lax.logistic(logits) - labels[...].astype(jnp.float32)
    column = jnp.transpose(jnp.broadcast_to(slope, (8, slope.shape[1])))[:, :1]
    w = weight[...].astype(jnp.float32)
    gk = global_slots(0, shared)
    gv = global_slots(BLOCK, shared)
    glob_k = jnp.zeros((GLOBAL * BLOCK, head_dim), jnp.float32)
    glob_v = jnp.zeros((GLOBAL * BLOCK, head_dim), jnp.float32)
    own = []
    for i in range(blocks):
        kk = near_slots(i, 0, k, prev, after, incoming, rand, blocks)
        kk = jnp.concatenate([kk, gk], axis=0)
        d = column[i * BLOCK : (i + 1) * BLOCK]
        g = (upstream[i].astype(jnp.float32) + d * w).astype(bf16)
        vv = near_slots(i, BLOCK, v, prev, after, incoming, rand, blocks)
        vv = jnp.concatenate([vv, gv], axis=0)
        p = probs[i]
        dp = mm(g, vv, NT)
        ds = (p * (dp - jnp.sum(p * dp, axis=1, keepdims=True)) * inv_sqrt).astype(bf16)
        grad_q[i] = mm(ds, kk, NN)
        dk = mm(ds, q[i], TN)
        dv = mm(p.astype(bf16), g, TN)
        for j in range(RAND):
            lo = (3 + j) * BLOCK
            at = rand[i, j] // blocks
            outgoing[at, :BLOCK] = dk[lo : lo + BLOCK].astype(bf16)
            outgoing[at, BLOCK : 2 * BLOCK] = dv[lo : lo + BLOCK].astype(bf16)
        glob_k = glob_k + dk[(3 + RAND) * BLOCK :]
        glob_v = glob_v + dv[(3 + RAND) * BLOCK :]
        own.append((dk[: 3 * BLOCK], dv[: 3 * BLOCK]))
    for which, acc in enumerate((acc_k, acc_v)):
        lo = which * BLOCK
        for i in range(blocks):
            total = own[i][which][BLOCK : 2 * BLOCK]
            if i < blocks - 1:
                total = total + own[i + 1][which][:BLOCK].astype(bf16).astype(jnp.float32)
            if i > 0:
                total = total + own[i - 1][which][2 * BLOCK :].astype(bf16).astype(jnp.float32)
            acc[i] = total
        to_prev[lo : lo + BLOCK] = own[0][which][:BLOCK].astype(bf16)
        to_next[lo : lo + BLOCK] = own[blocks - 1][which][2 * BLOCK :].astype(bf16)
    per_block = BLOCK // CHUNK
    for n in range(2 * GLOBAL):
        lo = (n // 2) * BLOCK
        rows = (glob_v if n % 2 else glob_k)[lo : lo + BLOCK].astype(bf16)
        outgoing[n * per_block : (n + 1) * per_block, 2 * BLOCK :] = rows.reshape(per_block, CHUNK, head_dim)


def gather_kernel(pick, acc_k, acc_v, back, from_prev, from_next, out_k, out_v):
    blocks = acc_k.shape[0]
    f32 = jnp.float32
    out_k[...] = acc_k[...]
    out_v[...] = acc_v[...]
    out_k[0] = out_k[0] + from_prev[:BLOCK].astype(f32)
    out_v[0] = out_v[0] + from_prev[BLOCK:].astype(f32)
    out_k[blocks - 1] = out_k[blocks - 1] + from_next[:BLOCK].astype(f32)
    out_v[blocks - 1] = out_v[blocks - 1] + from_next[BLOCK:].astype(f32)
    for r in range(back.shape[0]):
        at = pick[r]

        @pl.when(at >= 0)
        def _():
            out_k[at] = out_k[at] + back[r, :BLOCK].astype(f32)
            out_v[at] = out_v[at] + back[r, BLOCK : 2 * BLOCK].astype(f32)


def final_kernel(glob, me, acc_k, acc_v, shared, out_k, out_v):
    blocks = acc_k.shape[0]
    f32 = jnp.float32
    out_k[...] = acc_k[...]
    out_v[...] = acc_v[...]
    for g in range(GLOBAL):

        @pl.when(glob[g] // blocks == me[0])
        def _():
            at = glob[g] % blocks
            lo = g * 2 * BLOCK
            out_k[at] = out_k[at] + shared[lo : lo + BLOCK].astype(f32)
            out_v[at] = out_v[at] + shared[lo + BLOCK : lo + 2 * BLOCK].astype(f32)


def exchange(x, axis):
    return lax.all_to_all(x, axis, split_axis=0, concat_axis=0, tiled=True)


def body(queries, key_rows, value_rows, upstream, exit_weight, labels, rand_blocks, glob_blocks):
    tokens, head_dim = queries.shape
    blocks = tokens // BLOCK
    shards = lax.axis_size("seq")
    heads = lax.axis_size("head")
    myself = lax.axis_index("seq")
    bf16 = jnp.bfloat16
    f32 = jnp.float32
    keys = (3 + RAND + GLOBAL) * BLOCK
    wide = 2 * BLOCK
    ups = [(n, n + 1) for n in range(shards - 1)]
    downs = [(n + 1, n) for n in range(shards - 1)]

    me = jnp.stack([myself, jnp.full_like(myself, shards)])
    rand = lax.dynamic_slice_in_dim(rand_blocks, myself * blocks, blocks, 0)
    mine = jnp.where(rand_blocks // blocks == myself, rand_blocks % blocks, -1)
    pick = jnp.max(jnp.max(mine, axis=1).reshape(shards, blocks), axis=1)

    q = queries.reshape(blocks, BLOCK, head_dim)
    k = key_rows.reshape(blocks, BLOCK, head_dim)
    v = value_rows.reshape(blocks, BLOCK, head_dim)
    up = upstream.reshape(blocks, BLOCK, head_dim)
    weight = exit_weight.reshape(1, head_dim)
    slot_rows = wide + CHUNK
    acc3 = (blocks, BLOCK, head_dim)

    send, first, last = call(
        pack_kernel, "pack", 2, 2,
        [((shards, slot_rows, head_dim), bf16), ((wide, head_dim), bf16), ((wide, head_dim), bf16)],
        mib=None,
    )(pick, glob_blocks, k, v)
    incoming = exchange(send, "seq")
    prev = lax.ppermute(last, "seq", ups)
    after = lax.ppermute(first, "seq", downs)
    owner = glob_blocks[myself // (shards // GLOBAL)] // blocks
    piece = lax.dynamic_slice(incoming, (owner, wide, 0), (1, CHUNK, head_dim))
    shared = exchange(jnp.broadcast_to(piece, (shards, CHUNK, head_dim)), "seq")
    shared = shared.reshape(GLOBAL * wide, head_dim)

    near = (blocks, BLOCK, (3 + RAND) * BLOCK)
    terms, out, peak, total = call(
        near_kernel, "near", 2, 6, [(near, f32), (acc3, f32), (acc3, f32), (acc3, f32)]
    )(rand, me, q, k, v, prev, after, incoming)
    full = (blocks, BLOCK, keys)
    attended, probs, part = call(
        forward_kernel, "forward", 0, 7, [(acc3, bf16), (full, f32), ((heads, 1, tokens), f32)]
    )(q, shared, weight, terms, out, peak, total)
    parts = exchange(part, "head")

    grad_q, acc_k, acc_v, outgoing, to_prev, to_next = call(
        backward_kernel, "backward", 1, 12,
        [(acc3, f32), (acc3, f32), (acc3, f32), ((shards, slot_rows, head_dim), bf16),
         ((wide, head_dim), bf16), ((wide, head_dim), bf16)],
    )(
        rand, parts, labels.reshape(1, tokens), q, k, v, prev, after, incoming, shared, weight, up, probs
    )
    back = exchange(outgoing, "seq")
    from_prev = lax.ppermute(to_next, "seq", ups)
    from_next = lax.ppermute(to_prev, "seq", downs)
    gsum = jnp.sum(back[:, wide:].astype(f32), axis=0, keepdims=True).astype(bf16)
    gtotal = exchange(jnp.broadcast_to(gsum, (shards, CHUNK, head_dim)), "seq")
    gtotal = gtotal.reshape(GLOBAL * wide, head_dim)

    logits = jnp.sum(parts, axis=(0, 1))
    token_loss = jax.nn.softplus(logits) - labels.astype(f32) * logits

    acc_k, acc_v = call(gather_kernel, "gather", 1, 5, [(acc3, f32)] * 2)(
        pick, acc_k, acc_v, back, from_prev, from_next
    )
    out_k, out_v = call(final_kernel, "final", 2, 3, [(acc3, f32)] * 2)(
        glob_blocks, me, acc_k, acc_v, gtotal
    )
    flat = (tokens, head_dim)
    return (
        attended.reshape(flat),
        token_loss,
        grad_q.reshape(flat),
        out_k.reshape(flat),
        out_v.reshape(flat),
    )


def solution(mesh):
    placed = (
        P("seq", "head"),
        P("seq", "head"),
        P("seq", "head"),
        P("seq", "head"),
        P("head"),
        P("seq"),
        P(),
        P(),
    )
    return jax.shard_map(
        body,
        mesh=mesh,
        in_specs=placed,
        out_specs=(
            P("seq", "head"),
            P("seq"),
            P("seq", "head"),
            P("seq", "head"),
            P("seq", "head"),
        ),
        check_vma=False,
    )
```

```python
import math

import jax
import jax.numpy as jnp
from jax import lax
from jax.experimental import pallas as pl
from jax.experimental.pallas import tpu as pltpu
from jax.sharding import PartitionSpec as P

BLOCK = 64
RAND = 3
GLOBAL = 2
CHUNK = 8

NT = (((1,), (1,)), ((), ()))
NN = (((1,), (0,)), ((), ()))
TN = (((0,), (0,)), ((), ()))


def mm(a, b, dims):
    return lax.dot_general(a, b, dims, preferred_element_type=jnp.float32)


def smem(count):
    return [pl.BlockSpec(memory_space=pltpu.SMEM) for _ in range(count)]


def vmem(count):
    return [pl.BlockSpec(memory_space=pltpu.VMEM) for _ in range(count)]


def call(kernel, name, n_smem, n_vmem, outs, mib=40, **kw):
    if mib:
        kw["compiler_params"] = pltpu.CompilerParams(vmem_limit_bytes=mib * 1024 * 1024)
    return pl.pallas_call(
        kernel,
        name=name,
        in_specs=smem(n_smem) + vmem(n_vmem),
        out_specs=tuple(vmem(len(outs))),
        out_shape=tuple(jax.ShapeDtypeStruct(s, d) for s, d in outs),
        **kw,
    )


def pack_kernel(pick, glob, k, v, send, first, last):
    blocks = k.shape[0]
    wide = 2 * BLOCK
    per_block = BLOCK // CHUNK
    for r in range(send.shape[0]):
        at = jnp.maximum(pick[r], 0)
        send[r, :BLOCK] = k[at]
        send[r, BLOCK:wide] = v[at]
    for g in range(GLOBAL):
        at = glob[g] % blocks
        for n, src in enumerate((k, v)):
            rows = src[at].reshape(per_block, CHUNK, src.shape[2])
            lo = (2 * g + n) * per_block
            send[lo : lo + per_block, wide:] = rows
    first[:BLOCK] = k[0]
    first[BLOCK:] = v[0]
    last[:BLOCK] = k[blocks - 1]
    last[BLOCK:] = v[blocks - 1]


def near_slots(i, base, local, prev, after, incoming, rand, blocks):
    parts = [
        local[i - 1] if i > 0 else prev[base : base + BLOCK],
        local[i],
        local[i + 1] if i < blocks - 1 else after[base : base + BLOCK],
    ]
    for j in range(RAND):
        parts.append(incoming[rand[i, j] // blocks, base : base + BLOCK])
    return jnp.concatenate(parts, axis=0)


def global_slots(base, shared):
    lows = [g * 2 * BLOCK + base for g in range(GLOBAL)]
    return jnp.concatenate([shared[lo : lo + BLOCK] for lo in lows], axis=0)


def near_kernel(rand, me, q, k, v, prev, after, incoming, terms, out, peak, total):
    blocks = k.shape[0]
    head_dim = k.shape[2]
    keys = (3 + RAND) * BLOCK
    inv_sqrt = 1.0 / math.sqrt(head_dim)
    lane = lax.broadcasted_iota(jnp.int32, (BLOCK, keys), 1)
    for i in range(blocks):
        kk = near_slots(i, 0, k, prev, after, incoming, rand, blocks)
        vv = near_slots(i, BLOCK, v, prev, after, incoming, rand, blocks)
        s = mm(q[i], kk, NT) * inv_sqrt
        if i == 0:
            s = jnp.where((lane < BLOCK) & (me[0] == 0), -jnp.inf, s)
        if i == blocks - 1:
            void = (lane >= 2 * BLOCK) & (lane < 3 * BLOCK)
            s = jnp.where(void & (me[0] == me[1] - 1), -jnp.inf, s)
        m = jnp.max(s, axis=1, keepdims=True)
        e = jnp.exp(s - m)
        terms[i] = e
        out[i] = mm(e.astype(jnp.bfloat16), vv, NN)
        peak[i] = jnp.broadcast_to(m, (BLOCK, head_dim))
        total[i] = jnp.broadcast_to(jnp.sum(e, axis=1, keepdims=True), (BLOCK, head_dim))


def forward_kernel(q, shared, weight, terms, out, peak, total, attended, probs, part):
    blocks, _, head_dim = q.shape
    flat = (blocks * BLOCK, head_dim)
    inv_sqrt = 1.0 / math.sqrt(head_dim)
    w8 = jnp.broadcast_to(weight[...], (8, head_dim))
    s = mm(q[...].reshape(flat), global_slots(0, shared), NT) * inv_sqrt
    old = peak[...].reshape(flat)
    m = jnp.maximum(old, jnp.max(s, axis=1, keepdims=True))
    e = jnp.exp(s - m)
    shift = jnp.exp(old - m)
    inv = 1.0 / (shift * total[...].reshape(flat) + jnp.sum(e, axis=1, keepdims=True))
    scale = (shift * inv).reshape(blocks, BLOCK, head_dim)
    near = (3 + RAND) * BLOCK
    for lo in range(0, near, head_dim):
        probs[:, :, lo : lo + head_dim] = terms[:, :, lo : lo + head_dim] * scale
    probs[:, :, near:] = (e * inv).reshape(blocks, BLOCK, head_dim)
    a = out[...].reshape(flat) * shift + mm(e.astype(jnp.bfloat16), global_slots(BLOCK, shared), NN)
    a = (a * inv).astype(jnp.bfloat16)
    attended[...] = a.reshape(blocks, BLOCK, head_dim)
    row = mm(w8, a, NT)[:1]
    for r in range(part.shape[0]):
        part[r] = row


def backward_kernel(
    rand, parts, labels, q, k, v, prev, after, incoming, shared, weight, upstream, probs,
    grad_q, acc_k, acc_v, outgoing, to_prev, to_next,
):
    blocks = k.shape[0]
    head_dim = k.shape[2]
    inv_sqrt = 1.0 / math.sqrt(head_dim)
    bf16 = jnp.bfloat16
    logits = jnp.sum(parts[...], axis=0)
    slope = lax.logistic(logits) - labels[...].astype(jnp.float32)
    column = jnp.transpose(jnp.broadcast_to(slope, (8, slope.shape[1])))[:, :1]
    w = weight[...].astype(jnp.float32)
    gk = global_slots(0, shared)
    gv = global_slots(BLOCK, shared)
    glob_k = jnp.zeros((GLOBAL * BLOCK, head_dim), jnp.float32)
    glob_v = jnp.zeros((GLOBAL * BLOCK, head_dim), jnp.float32)
    none = jnp.zeros((BLOCK, head_dim), bf16)
    own = []
    for i in range(blocks):
        kk = near_slots(i, 0, k, prev, after, incoming, rand, blocks)
        kk = jnp.concatenate([kk, gk], axis=0)
        d = column[i * BLOCK : (i + 1) * BLOCK]
        g = (upstream[i].astype(jnp.float32) + d * w).astype(bf16)
        vv = near_slots(i, BLOCK, v, prev, after, incoming, rand, blocks)
        vv = jnp.concatenate([vv, gv], axis=0)
        p = probs[i]
        dp = mm(g, vv, NT)
        ds = (p * (dp - jnp.sum(p * dp, axis=1, keepdims=True)) * inv_sqrt).astype(bf16)
        grad_q[i] = mm(ds, kk, NN)
        left = jnp.concatenate([ds, p.astype(bf16)], axis=0)
        right = jnp.concatenate(
            [jnp.concatenate([q[i], none], axis=1), jnp.concatenate([none, g], axis=1)], axis=0
        )
        both = mm(left, right, TN)
        dk = both[:, :head_dim]
        dv = both[:, head_dim:]
        for j in range(RAND):
            lo = (3 + j) * BLOCK
            at = rand[i, j] // blocks
            outgoing[at, :BLOCK] = dk[lo : lo + BLOCK].astype(bf16)
            outgoing[at, BLOCK : 2 * BLOCK] = dv[lo : lo + BLOCK].astype(bf16)
        glob_k = glob_k + dk[(3 + RAND) * BLOCK :]
        glob_v = glob_v + dv[(3 + RAND) * BLOCK :]
        own.append((dk[: 3 * BLOCK], dv[: 3 * BLOCK]))
    for which, acc in enumerate((acc_k, acc_v)):
        lo = which * BLOCK
        for i in range(blocks):
            total = own[i][which][BLOCK : 2 * BLOCK]
            if i < blocks - 1:
                total = total + own[i + 1][which][:BLOCK].astype(bf16).astype(jnp.float32)
            if i > 0:
                total = total + own[i - 1][which][2 * BLOCK :].astype(bf16).astype(jnp.float32)
            acc[i] = total
        to_prev[lo : lo + BLOCK] = own[0][which][:BLOCK].astype(bf16)
        to_next[lo : lo + BLOCK] = own[blocks - 1][which][2 * BLOCK :].astype(bf16)
    per_block = BLOCK // CHUNK
    for n in range(2 * GLOBAL):
        lo = (n // 2) * BLOCK
        rows = (glob_v if n % 2 else glob_k)[lo : lo + BLOCK].astype(bf16)
        outgoing[n * per_block : (n + 1) * per_block, 2 * BLOCK :] = rows.reshape(per_block, CHUNK, head_dim)


def gather_kernel(pick, acc_k, acc_v, back, from_prev, from_next, out_k, out_v):
    blocks = acc_k.shape[0]
    f32 = jnp.float32
    out_k[...] = acc_k[...]
    out_v[...] = acc_v[...]
    out_k[0] = out_k[0] + from_prev[:BLOCK].astype(f32)
    out_v[0] = out_v[0] + from_prev[BLOCK:].astype(f32)
    out_k[blocks - 1] = out_k[blocks - 1] + from_next[:BLOCK].astype(f32)
    out_v[blocks - 1] = out_v[blocks - 1] + from_next[BLOCK:].astype(f32)
    for r in range(back.shape[0]):
        at = pick[r]

        @pl.when(at >= 0)
        def _():
            out_k[at] = out_k[at] + back[r, :BLOCK].astype(f32)
            out_v[at] = out_v[at] + back[r, BLOCK : 2 * BLOCK].astype(f32)


def final_kernel(glob, me, acc_k, acc_v, shared, out_k, out_v):
    blocks = acc_k.shape[0]
    f32 = jnp.float32
    out_k[...] = acc_k[...]
    out_v[...] = acc_v[...]
    for g in range(GLOBAL):

        @pl.when(glob[g] // blocks == me[0])
        def _():
            at = glob[g] % blocks
            lo = g * 2 * BLOCK
            out_k[at] = out_k[at] + shared[lo : lo + BLOCK].astype(f32)
            out_v[at] = out_v[at] + shared[lo + BLOCK : lo + 2 * BLOCK].astype(f32)


def exchange(x, axis):
    return lax.all_to_all(x, axis, split_axis=0, concat_axis=0, tiled=True)


def body(queries, key_rows, value_rows, upstream, exit_weight, labels, rand_blocks, glob_blocks):
    tokens, head_dim = queries.shape
    blocks = tokens // BLOCK
    shards = lax.axis_size("seq")
    heads = lax.axis_size("head")
    myself = lax.axis_index("seq")
    bf16 = jnp.bfloat16
    f32 = jnp.float32
    keys = (3 + RAND + GLOBAL) * BLOCK
    wide = 2 * BLOCK
    ups = [(n, n + 1) for n in range(shards - 1)]
    downs = [(n + 1, n) for n in range(shards - 1)]

    me = jnp.stack([myself, jnp.full_like(myself, shards)])
    rand = lax.dynamic_slice_in_dim(rand_blocks, myself * blocks, blocks, 0)
    mine = jnp.where(rand_blocks // blocks == myself, rand_blocks % blocks, -1)
    pick = jnp.max(jnp.max(mine, axis=1).reshape(shards, blocks), axis=1)

    q = queries.reshape(blocks, BLOCK, head_dim)
    k = key_rows.reshape(blocks, BLOCK, head_dim)
    v = value_rows.reshape(blocks, BLOCK, head_dim)
    up = upstream.reshape(blocks, BLOCK, head_dim)
    weight = exit_weight.reshape(1, head_dim)
    slot_rows = wide + CHUNK
    acc3 = (blocks, BLOCK, head_dim)

    send, first, last = call(
        pack_kernel, "pack", 2, 2,
        [((shards, slot_rows, head_dim), bf16), ((wide, head_dim), bf16), ((wide, head_dim), bf16)],
        mib=None,
    )(pick, glob_blocks, k, v)
    incoming = exchange(send, "seq")
    prev = lax.ppermute(last, "seq", ups)
    after = lax.ppermute(first, "seq", downs)
    owner = glob_blocks[myself // (shards // GLOBAL)] // blocks
    piece = lax.dynamic_slice(incoming, (owner, wide, 0), (1, CHUNK, head_dim))
    shared = exchange(jnp.broadcast_to(piece, (shards, CHUNK, head_dim)), "seq")
    shared = shared.reshape(GLOBAL * wide, head_dim)

    near = (blocks, BLOCK, (3 + RAND) * BLOCK)
    terms, out, peak, total = call(
        near_kernel, "near", 2, 6, [(near, f32), (acc3, f32), (acc3, f32), (acc3, f32)]
    )(rand, me, q, k, v, prev, after, incoming)
    full = (blocks, BLOCK, keys)
    attended, probs, part = call(
        forward_kernel, "forward", 0, 7, [(acc3, bf16), (full, f32), ((heads, 1, tokens), f32)]
    )(q, shared, weight, terms, out, peak, total)
    parts = exchange(part, "head")

    grad_q, acc_k, acc_v, outgoing, to_prev, to_next = call(
        backward_kernel, "backward", 1, 12,
        [(acc3, f32), (acc3, f32), (acc3, f32), ((shards, slot_rows, head_dim), bf16),
         ((wide, head_dim), bf16), ((wide, head_dim), bf16)],
    )(
        rand, parts, labels.reshape(1, tokens), q, k, v, prev, after, incoming, shared, weight, up, probs
    )
    back = exchange(outgoing, "seq")
    from_prev = lax.ppermute(to_next, "seq", ups)
    from_next = lax.ppermute(to_prev, "seq", downs)
    gsum = jnp.sum(back[:, wide:].astype(f32), axis=0, keepdims=True).astype(bf16)
    gtotal = exchange(jnp.broadcast_to(gsum, (shards, CHUNK, head_dim)), "seq")
    gtotal = gtotal.reshape(GLOBAL * wide, head_dim)

    logits = jnp.sum(parts, axis=(0, 1))
    token_loss = jax.nn.softplus(logits) - labels.astype(f32) * logits

    acc_k, acc_v = call(gather_kernel, "gather", 1, 5, [(acc3, f32)] * 2)(
        pick, acc_k, acc_v, back, from_prev, from_next
    )
    out_k, out_v = call(final_kernel, "final", 2, 3, [(acc3, f32)] * 2)(
        glob_blocks, me, acc_k, acc_v, gtotal
    )
    flat = (tokens, head_dim)
    return (
        attended.reshape(flat),
        token_loss,
        grad_q.reshape(flat),
        out_k.reshape(flat),
        out_v.reshape(flat),
    )


def solution(mesh):
    placed = (
        P("seq", "head"),
        P("seq", "head"),
        P("seq", "head"),
        P("seq", "head"),
        P("head"),
        P("seq"),
        P(),
        P(),
    )
    return jax.shard_map(
        body,
        mesh=mesh,
        in_specs=placed,
        out_specs=(
            P("seq", "head"),
            P("seq"),
            P("seq", "head"),
            P("seq", "head"),
            P("seq", "head"),
        ),
        check_vma=False,
    )
```

```python
import math

import jax
import jax.numpy as jnp
from jax import lax
from jax.experimental import pallas as pl
from jax.experimental.pallas import tpu as pltpu
from jax.sharding import PartitionSpec as P

BLOCK = 64
RAND = 3
GLOBAL = 2
CHUNK = 8

NT = (((1,), (1,)), ((), ()))
NN = (((1,), (0,)), ((), ()))
TN = (((0,), (0,)), ((), ()))


def mm(a, b, dims):
    return lax.dot_general(a, b, dims, preferred_element_type=jnp.float32)


def smem(count):
    return [pl.BlockSpec(memory_space=pltpu.SMEM) for _ in range(count)]


def vmem(count):
    return [pl.BlockSpec(memory_space=pltpu.VMEM) for _ in range(count)]


def call(kernel, name, n_smem, n_vmem, outs, mib=40, **kw):
    if mib:
        kw["compiler_params"] = pltpu.CompilerParams(vmem_limit_bytes=mib * 1024 * 1024)
    return pl.pallas_call(
        kernel,
        name=name,
        in_specs=smem(n_smem) + vmem(n_vmem),
        out_specs=tuple(vmem(len(outs))),
        out_shape=tuple(jax.ShapeDtypeStruct(s, d) for s, d in outs),
        **kw,
    )


def pack_kernel(pick, glob, k, v, send, first, last):
    blocks = k.shape[0]
    wide = 2 * BLOCK
    per_block = BLOCK // CHUNK
    for r in range(send.shape[0]):
        at = jnp.maximum(pick[r], 0)
        send[r, :BLOCK] = k[at]
        send[r, BLOCK:wide] = v[at]
    for g in range(GLOBAL):
        at = glob[g] % blocks
        for n, src in enumerate((k, v)):
            rows = src[at].reshape(per_block, CHUNK, src.shape[2])
            lo = (2 * g + n) * per_block
            send[lo : lo + per_block, wide:] = rows
    first[:BLOCK] = k[0]
    first[BLOCK:] = v[0]
    last[:BLOCK] = k[blocks - 1]
    last[BLOCK:] = v[blocks - 1]


def near_slots(i, base, local, prev, after, incoming, rand, blocks):
    parts = [
        local[i - 1] if i > 0 else prev[base : base + BLOCK],
        local[i],
        local[i + 1] if i < blocks - 1 else after[base : base + BLOCK],
    ]
    for j in range(RAND):
        parts.append(incoming[rand[i, j] // blocks, base : base + BLOCK])
    return jnp.concatenate(parts, axis=0)


def global_slots(base, shared):
    lows = [g * 2 * BLOCK + base for g in range(GLOBAL)]
    return jnp.concatenate([shared[lo : lo + BLOCK] for lo in lows], axis=0)


def near_kernel(rand, me, q, k, v, prev, after, incoming, terms, out, peak, total):
    blocks = k.shape[0]
    head_dim = k.shape[2]
    keys = (3 + RAND) * BLOCK
    inv_sqrt = 1.0 / math.sqrt(head_dim)
    lane = lax.broadcasted_iota(jnp.int32, (BLOCK, keys), 1)
    for i in range(blocks):
        kk = near_slots(i, 0, k, prev, after, incoming, rand, blocks)
        vv = near_slots(i, BLOCK, v, prev, after, incoming, rand, blocks)
        s = mm(q[i], kk, NT) * inv_sqrt
        if i == 0:
            s = jnp.where((lane < BLOCK) & (me[0] == 0), -jnp.inf, s)
        if i == blocks - 1:
            void = (lane >= 2 * BLOCK) & (lane < 3 * BLOCK)
            s = jnp.where(void & (me[0] == me[1] - 1), -jnp.inf, s)
        m = jnp.max(s, axis=1, keepdims=True)
        e = jnp.exp(s - m)
        terms[i] = e
        out[i] = mm(e.astype(jnp.bfloat16), vv, NN)
        peak[i] = jnp.broadcast_to(m, (BLOCK, head_dim))
        total[i] = jnp.broadcast_to(jnp.sum(e, axis=1, keepdims=True), (BLOCK, head_dim))


def forward_kernel(q, shared, weight, terms, out, peak, total, attended, probs, part):
    blocks, _, head_dim = q.shape
    flat = (blocks * BLOCK, head_dim)
    inv_sqrt = 1.0 / math.sqrt(head_dim)
    w8 = jnp.broadcast_to(weight[...], (8, head_dim))
    s = mm(q[...].reshape(flat), global_slots(0, shared), NT) * inv_sqrt
    old = peak[...].reshape(flat)
    m = jnp.maximum(old, jnp.max(s, axis=1, keepdims=True))
    e = jnp.exp(s - m)
    shift = jnp.exp(old - m)
    inv = 1.0 / (shift * total[...].reshape(flat) + jnp.sum(e, axis=1, keepdims=True))
    scale = (shift * inv).reshape(blocks, BLOCK, head_dim)
    near = (3 + RAND) * BLOCK
    for lo in range(0, near, head_dim):
        probs[:, :, lo : lo + head_dim] = terms[:, :, lo : lo + head_dim] * scale
    probs[:, :, near:] = (e * inv).reshape(blocks, BLOCK, head_dim)
    a = out[...].reshape(flat) * shift + mm(e.astype(jnp.bfloat16), global_slots(BLOCK, shared), NN)
    a = (a * inv).astype(jnp.bfloat16)
    attended[...] = a.reshape(blocks, BLOCK, head_dim)
    row = mm(w8, a, NT)[:1]
    for r in range(part.shape[0]):
        part[r] = row


def backward_kernel(
    rand, parts, labels, q, k, v, prev, after, incoming, shared, weight, upstream, probs,
    grad_q, acc_k, acc_v, outgoing, to_prev, to_next,
):
    blocks = k.shape[0]
    head_dim = k.shape[2]
    inv_sqrt = 1.0 / math.sqrt(head_dim)
    bf16 = jnp.bfloat16
    logits = jnp.sum(parts[...], axis=0)
    slope = lax.logistic(logits) - labels[...].astype(jnp.float32)
    column = jnp.transpose(jnp.broadcast_to(slope, (8, slope.shape[1])))[:, :1]
    w = weight[...].astype(jnp.float32)
    gk = global_slots(0, shared)
    gv = global_slots(BLOCK, shared)
    glob_k = jnp.zeros((GLOBAL * BLOCK, head_dim), jnp.float32)
    glob_v = jnp.zeros((GLOBAL * BLOCK, head_dim), jnp.float32)
    none = jnp.zeros((BLOCK, head_dim), bf16)
    own = []
    for i in range(blocks):
        kk = near_slots(i, 0, k, prev, after, incoming, rand, blocks)
        kk = jnp.concatenate([kk, gk], axis=0)
        d = column[i * BLOCK : (i + 1) * BLOCK]
        g = (upstream[i].astype(jnp.float32) + d * w).astype(bf16)
        vv = near_slots(i, BLOCK, v, prev, after, incoming, rand, blocks)
        vv = jnp.concatenate([vv, gv], axis=0)
        p = probs[i]
        dp = mm(g, vv, NT)
        ds = (p * (dp - jnp.sum(p * dp, axis=1, keepdims=True)) * inv_sqrt).astype(bf16)
        grad_q[i] = mm(ds, kk, NN)
        left = jnp.concatenate([ds, p.astype(bf16)], axis=0)
        right = jnp.concatenate(
            [jnp.concatenate([q[i], none], axis=1), jnp.concatenate([none, g], axis=1)], axis=0
        )
        both = mm(left, right, TN)
        dk = both[:, :head_dim]
        dv = both[:, head_dim:]
        for j in range(RAND):
            lo = (3 + j) * BLOCK
            at = rand[i, j] // blocks
            outgoing[at, :BLOCK] = dk[lo : lo + BLOCK].astype(bf16)
            outgoing[at, BLOCK : 2 * BLOCK] = dv[lo : lo + BLOCK].astype(bf16)
        glob_k = glob_k + dk[(3 + RAND) * BLOCK :]
        glob_v = glob_v + dv[(3 + RAND) * BLOCK :]
        own.append((dk[: 3 * BLOCK], dv[: 3 * BLOCK]))
    for which, acc in enumerate((acc_k, acc_v)):
        lo = which * BLOCK
        for i in range(blocks):
            total = own[i][which][BLOCK : 2 * BLOCK]
            if i < blocks - 1:
                total = total + own[i + 1][which][:BLOCK].astype(bf16).astype(jnp.float32)
            if i > 0:
                total = total + own[i - 1][which][2 * BLOCK :].astype(bf16).astype(jnp.float32)
            acc[i] = total
        to_prev[lo : lo + BLOCK] = own[0][which][:BLOCK].astype(bf16)
        to_next[lo : lo + BLOCK] = own[blocks - 1][which][2 * BLOCK :].astype(bf16)
    per_block = BLOCK // CHUNK
    for n in range(2 * GLOBAL):
        lo = (n // 2) * BLOCK
        rows = (glob_v if n % 2 else glob_k)[lo : lo + BLOCK].astype(bf16)
        outgoing[n * per_block : (n + 1) * per_block, 2 * BLOCK :] = rows.reshape(per_block, CHUNK, head_dim)


def gather_kernel(pick, glob, acc_k, acc_v, back, from_prev, from_next, out_k, out_v, held):
    blocks = acc_k.shape[0]
    f32 = jnp.float32
    out_k[...] = acc_k[...]
    out_v[...] = acc_v[...]
    out_k[0] = out_k[0] + from_prev[:BLOCK].astype(f32)
    out_v[0] = out_v[0] + from_prev[BLOCK:].astype(f32)
    out_k[blocks - 1] = out_k[blocks - 1] + from_next[:BLOCK].astype(f32)
    out_v[blocks - 1] = out_v[blocks - 1] + from_next[BLOCK:].astype(f32)
    for r in range(back.shape[0]):
        at = pick[r]

        @pl.when(at >= 0)
        def _():
            out_k[at] = out_k[at] + back[r, :BLOCK].astype(f32)
            out_v[at] = out_v[at] + back[r, BLOCK : 2 * BLOCK].astype(f32)

    for g in range(GLOBAL):
        at = glob[g] % blocks
        held[2 * g] = out_k[at]
        held[2 * g + 1] = out_v[at]


def final_kernel(glob, me, held, shared, in_k, in_v, out_k, out_v, summed, sems):
    del in_k, in_v
    blocks = out_k.shape[0]
    for g in range(GLOBAL):

        @pl.when(glob[g] // blocks == me[0])
        def _():
            copies = []
            for n, out in enumerate((out_k, out_v)):
                slot = 2 * g + n
                rows = shared[slot * BLOCK : (slot + 1) * BLOCK].astype(jnp.float32)
                summed[slot] = held[slot] + rows
                target = out.at[glob[g] % blocks]
                copies.append(pltpu.make_async_copy(summed.at[slot], target, sems.at[slot]))
                copies[-1].start()
            for copy in copies:
                copy.wait()


def exchange(x, axis):
    return lax.all_to_all(x, axis, split_axis=0, concat_axis=0, tiled=True)


def body(queries, key_rows, value_rows, upstream, exit_weight, labels, rand_blocks, glob_blocks):
    tokens, head_dim = queries.shape
    blocks = tokens // BLOCK
    shards = lax.axis_size("seq")
    heads = lax.axis_size("head")
    myself = lax.axis_index("seq")
    bf16 = jnp.bfloat16
    f32 = jnp.float32
    keys = (3 + RAND + GLOBAL) * BLOCK
    wide = 2 * BLOCK
    ups = [(n, n + 1) for n in range(shards - 1)]
    downs = [(n + 1, n) for n in range(shards - 1)]

    me = jnp.stack([myself, jnp.full_like(myself, shards)])
    rand = lax.dynamic_slice_in_dim(rand_blocks, myself * blocks, blocks, 0)
    mine = jnp.where(rand_blocks // blocks == myself, rand_blocks % blocks, -1)
    pick = jnp.max(jnp.max(mine, axis=1).reshape(shards, blocks), axis=1)

    q = queries.reshape(blocks, BLOCK, head_dim)
    k = key_rows.reshape(blocks, BLOCK, head_dim)
    v = value_rows.reshape(blocks, BLOCK, head_dim)
    up = upstream.reshape(blocks, BLOCK, head_dim)
    weight = exit_weight.reshape(1, head_dim)
    slot_rows = wide + CHUNK
    acc3 = (blocks, BLOCK, head_dim)

    send, first, last = call(
        pack_kernel, "pack", 2, 2,
        [((shards, slot_rows, head_dim), bf16), ((wide, head_dim), bf16), ((wide, head_dim), bf16)],
        mib=None,
    )(pick, glob_blocks, k, v)
    incoming = exchange(send, "seq")
    prev = lax.ppermute(last, "seq", ups)
    after = lax.ppermute(first, "seq", downs)
    owner = glob_blocks[myself // (shards // GLOBAL)] // blocks
    piece = lax.dynamic_slice(incoming, (owner, wide, 0), (1, CHUNK, head_dim))
    shared = exchange(jnp.broadcast_to(piece, (shards, CHUNK, head_dim)), "seq")
    shared = shared.reshape(GLOBAL * wide, head_dim)

    near = (blocks, BLOCK, (3 + RAND) * BLOCK)
    terms, out, peak, total = call(
        near_kernel, "near", 2, 6, [(near, f32), (acc3, f32), (acc3, f32), (acc3, f32)]
    )(rand, me, q, k, v, prev, after, incoming)
    full = (blocks, BLOCK, keys)
    attended, probs, part = call(
        forward_kernel, "forward", 0, 7, [(acc3, bf16), (full, f32), ((heads, 1, tokens), f32)]
    )(q, shared, weight, terms, out, peak, total)
    parts = exchange(part, "head")

    grad_q, acc_k, acc_v, outgoing, to_prev, to_next = call(
        backward_kernel, "backward", 1, 12,
        [(acc3, f32), (acc3, f32), (acc3, f32), ((shards, slot_rows, head_dim), bf16),
         ((wide, head_dim), bf16), ((wide, head_dim), bf16)],
    )(
        rand, parts, labels.reshape(1, tokens), q, k, v, prev, after, incoming, shared, weight, up, probs
    )
    back = exchange(outgoing, "seq")
    from_prev = lax.ppermute(to_next, "seq", ups)
    from_next = lax.ppermute(to_prev, "seq", downs)
    gsum = jnp.sum(back[:, wide:].astype(f32), axis=0, keepdims=True).astype(bf16)
    gtotal = exchange(jnp.broadcast_to(gsum, (shards, CHUNK, head_dim)), "seq")
    gtotal = gtotal.reshape(GLOBAL * wide, head_dim)

    logits = jnp.sum(parts, axis=(0, 1))
    token_loss = jax.nn.softplus(logits) - labels.astype(f32) * logits

    anywhere = pl.BlockSpec(memory_space=pl.ANY)
    held3 = (2 * GLOBAL, BLOCK, head_dim)
    out_k, out_v, held = call(
        gather_kernel, "gather", 2, 5, [(acc3, f32), (acc3, f32), (held3, f32)]
    )(pick, glob_blocks, acc_k, acc_v, back, from_prev, from_next)
    out_k, out_v = pl.pallas_call(
        final_kernel,
        name="final",
        in_specs=smem(2) + vmem(2) + [anywhere] * 2,
        out_specs=(anywhere,) * 2,
        out_shape=(jax.ShapeDtypeStruct(acc3, f32),) * 2,
        scratch_shapes=[pltpu.VMEM(held3, f32), pltpu.SemaphoreType.DMA((2 * GLOBAL,))],
        input_output_aliases={4: 0, 5: 1},
        compiler_params=pltpu.CompilerParams(vmem_limit_bytes=4 * 1024 * 1024),
    )(glob_blocks, me, held, gtotal, out_k, out_v)
    flat = (tokens, head_dim)
    return (
        attended.reshape(flat),
        token_loss,
        grad_q.reshape(flat),
        out_k.reshape(flat),
        out_v.reshape(flat),
    )


def solution(mesh):
    placed = (
        P("seq", "head"),
        P("seq", "head"),
        P("seq", "head"),
        P("seq", "head"),
        P("head"),
        P("seq"),
        P(),
        P(),
    )
    return jax.shard_map(
        body,
        mesh=mesh,
        in_specs=placed,
        out_specs=(
            P("seq", "head"),
            P("seq"),
            P("seq", "head"),
            P("seq", "head"),
            P("seq", "head"),
        ),
        check_vma=False,
    )
```

```python
import math

import jax
import jax.numpy as jnp
from jax import lax
from jax.experimental import pallas as pl
from jax.experimental.pallas import tpu as pltpu
from jax.sharding import PartitionSpec as P

BLOCK = 64
RAND = 3
GLOBAL = 2
CHUNK = 8

NT = (((1,), (1,)), ((), ()))
NN = (((1,), (0,)), ((), ()))
TN = (((0,), (0,)), ((), ()))


def mm(a, b, dims):
    return lax.dot_general(a, b, dims, preferred_element_type=jnp.float32)


def smem(count):
    return [pl.BlockSpec(memory_space=pltpu.SMEM) for _ in range(count)]


def vmem(count):
    return [pl.BlockSpec(memory_space=pltpu.VMEM) for _ in range(count)]


def call(kernel, name, n_smem, n_vmem, outs, mib=40, **kw):
    if mib:
        kw["compiler_params"] = pltpu.CompilerParams(vmem_limit_bytes=mib * 1024 * 1024)
    return pl.pallas_call(
        kernel,
        name=name,
        in_specs=smem(n_smem) + vmem(n_vmem),
        out_specs=tuple(vmem(len(outs))),
        out_shape=tuple(jax.ShapeDtypeStruct(s, d) for s, d in outs),
        **kw,
    )


def pack_kernel(pick, glob, k, v, send, first, last):
    blocks = k.shape[0]
    wide = 2 * BLOCK
    per_block = BLOCK // CHUNK
    for r in range(send.shape[0]):
        at = jnp.maximum(pick[r], 0)
        send[r, :BLOCK] = k[at]
        send[r, BLOCK:wide] = v[at]
    for g in range(GLOBAL):
        at = glob[g] % blocks
        for n, src in enumerate((k, v)):
            rows = src[at].reshape(per_block, CHUNK, src.shape[2])
            lo = (2 * g + n) * per_block
            send[lo : lo + per_block, wide:] = rows
    first[:BLOCK] = k[0]
    first[BLOCK:] = v[0]
    last[:BLOCK] = k[blocks - 1]
    last[BLOCK:] = v[blocks - 1]


def near_slots(i, base, local, prev, after, incoming, rand, blocks):
    parts = [
        local[i - 1] if i > 0 else prev[base : base + BLOCK],
        local[i],
        local[i + 1] if i < blocks - 1 else after[base : base + BLOCK],
    ]
    for j in range(RAND):
        parts.append(incoming[rand[i, j] // blocks, base : base + BLOCK])
    return jnp.concatenate(parts, axis=0)


def global_slots(base, shared):
    lows = [g * 2 * BLOCK + base for g in range(GLOBAL)]
    return jnp.concatenate([shared[lo : lo + BLOCK] for lo in lows], axis=0)


def near_kernel(rand, me, q, k, v, prev, after, incoming, terms, out, peak, total):
    blocks = k.shape[0]
    head_dim = k.shape[2]
    keys = (3 + RAND) * BLOCK
    inv_sqrt = 1.0 / math.sqrt(head_dim)
    lane = lax.broadcasted_iota(jnp.int32, (BLOCK, keys), 1)
    for i in range(blocks):
        kk = near_slots(i, 0, k, prev, after, incoming, rand, blocks)
        vv = near_slots(i, BLOCK, v, prev, after, incoming, rand, blocks)
        s = mm(q[i], kk, NT) * inv_sqrt
        if i == 0:
            s = jnp.where((lane < BLOCK) & (me[0] == 0), -jnp.inf, s)
        if i == blocks - 1:
            void = (lane >= 2 * BLOCK) & (lane < 3 * BLOCK)
            s = jnp.where(void & (me[0] == me[1] - 1), -jnp.inf, s)
        m = jnp.max(s, axis=1, keepdims=True)
        e = jnp.exp(s - m)
        terms[i] = e
        out[i] = mm(e.astype(jnp.bfloat16), vv, NN)
        peak[i] = jnp.broadcast_to(m, (BLOCK, head_dim))
        total[i] = jnp.broadcast_to(jnp.sum(e, axis=1, keepdims=True), (BLOCK, head_dim))


def forward_kernel(q, shared, weight, terms, out, peak, total, attended, mean, probs, part):
    blocks, _, head_dim = q.shape
    flat = (blocks * BLOCK, head_dim)
    inv_sqrt = 1.0 / math.sqrt(head_dim)
    w8 = jnp.broadcast_to(weight[...], (8, head_dim))
    s = mm(q[...].reshape(flat), global_slots(0, shared), NT) * inv_sqrt
    old = peak[...].reshape(flat)
    m = jnp.maximum(old, jnp.max(s, axis=1, keepdims=True))
    e = jnp.exp(s - m)
    shift = jnp.exp(old - m)
    inv = 1.0 / (shift * total[...].reshape(flat) + jnp.sum(e, axis=1, keepdims=True))
    scale = (shift * inv).reshape(blocks, BLOCK, head_dim)
    near = (3 + RAND) * BLOCK
    for lo in range(0, near, head_dim):
        probs[:, :, lo : lo + head_dim] = terms[:, :, lo : lo + head_dim] * scale
    probs[:, :, near:] = (e * inv).reshape(blocks, BLOCK, head_dim)
    a = out[...].reshape(flat) * shift + mm(e.astype(jnp.bfloat16), global_slots(BLOCK, shared), NN)
    a = a * inv
    mean[...] = a.reshape(blocks, BLOCK, head_dim)
    a = a.astype(jnp.bfloat16)
    attended[...] = a.reshape(blocks, BLOCK, head_dim)
    row = mm(w8, a, NT)[:1]
    for r in range(part.shape[0]):
        part[r] = row


def backward_kernel(
    rand, parts, labels, q, k, v, prev, after, incoming, shared, weight, upstream, mean, probs,
    grad_q, acc_k, acc_v, outgoing, to_prev, to_next,
):
    blocks = k.shape[0]
    head_dim = k.shape[2]
    inv_sqrt = 1.0 / math.sqrt(head_dim)
    bf16 = jnp.bfloat16
    logits = jnp.sum(parts[...], axis=0)
    slope = lax.logistic(logits) - labels[...].astype(jnp.float32)
    column = jnp.transpose(jnp.broadcast_to(slope, (8, slope.shape[1])))[:, :1]
    w = weight[...].astype(jnp.float32)
    gk = global_slots(0, shared)
    gv = global_slots(BLOCK, shared)
    glob_k = jnp.zeros((GLOBAL * BLOCK, head_dim), jnp.float32)
    glob_v = jnp.zeros((GLOBAL * BLOCK, head_dim), jnp.float32)
    none = jnp.zeros((BLOCK, head_dim), bf16)
    own = []
    for i in range(blocks):
        kk = near_slots(i, 0, k, prev, after, incoming, rand, blocks)
        kk = jnp.concatenate([kk, gk], axis=0)
        d = column[i * BLOCK : (i + 1) * BLOCK]
        g = (upstream[i].astype(jnp.float32) + d * w).astype(bf16)
        vv = near_slots(i, BLOCK, v, prev, after, incoming, rand, blocks)
        vv = jnp.concatenate([vv, gv], axis=0)
        p = probs[i]
        dp = mm(g, vv, NT)
        dot = jnp.sum(g.astype(jnp.float32) * mean[i], axis=1, keepdims=True)
        ds = (p * (dp - dot) * inv_sqrt).astype(bf16)
        grad_q[i] = mm(ds, kk, NN)
        left = jnp.concatenate([ds, p.astype(bf16)], axis=0)
        right = jnp.concatenate(
            [jnp.concatenate([q[i], none], axis=1), jnp.concatenate([none, g], axis=1)], axis=0
        )
        both = mm(left, right, TN)
        dk = both[:, :head_dim]
        dv = both[:, head_dim:]
        for j in range(RAND):
            lo = (3 + j) * BLOCK
            at = rand[i, j] // blocks
            outgoing[at, :BLOCK] = dk[lo : lo + BLOCK].astype(bf16)
            outgoing[at, BLOCK : 2 * BLOCK] = dv[lo : lo + BLOCK].astype(bf16)
        glob_k = glob_k + dk[(3 + RAND) * BLOCK :]
        glob_v = glob_v + dv[(3 + RAND) * BLOCK :]
        own.append((dk[: 3 * BLOCK], dv[: 3 * BLOCK]))
    for which, acc in enumerate((acc_k, acc_v)):
        lo = which * BLOCK
        for i in range(blocks):
            total = own[i][which][BLOCK : 2 * BLOCK]
            if i < blocks - 1:
                total = total + own[i + 1][which][:BLOCK].astype(bf16).astype(jnp.float32)
            if i > 0:
                total = total + own[i - 1][which][2 * BLOCK :].astype(bf16).astype(jnp.float32)
            acc[i] = total
        to_prev[lo : lo + BLOCK] = own[0][which][:BLOCK].astype(bf16)
        to_next[lo : lo + BLOCK] = own[blocks - 1][which][2 * BLOCK :].astype(bf16)
    per_block = BLOCK // CHUNK
    for n in range(2 * GLOBAL):
        lo = (n // 2) * BLOCK
        rows = (glob_v if n % 2 else glob_k)[lo : lo + BLOCK].astype(bf16)
        outgoing[n * per_block : (n + 1) * per_block, 2 * BLOCK :] = rows.reshape(per_block, CHUNK, head_dim)


def gather_kernel(pick, glob, acc_k, acc_v, back, from_prev, from_next, out_k, out_v, held):
    blocks = acc_k.shape[0]
    f32 = jnp.float32
    out_k[...] = acc_k[...]
    out_v[...] = acc_v[...]
    out_k[0] = out_k[0] + from_prev[:BLOCK].astype(f32)
    out_v[0] = out_v[0] + from_prev[BLOCK:].astype(f32)
    out_k[blocks - 1] = out_k[blocks - 1] + from_next[:BLOCK].astype(f32)
    out_v[blocks - 1] = out_v[blocks - 1] + from_next[BLOCK:].astype(f32)
    for r in range(back.shape[0]):
        at = pick[r]

        @pl.when(at >= 0)
        def _():
            out_k[at] = out_k[at] + back[r, :BLOCK].astype(f32)
            out_v[at] = out_v[at] + back[r, BLOCK : 2 * BLOCK].astype(f32)

    for g in range(GLOBAL):
        at = glob[g] % blocks
        held[2 * g] = out_k[at]
        held[2 * g + 1] = out_v[at]


def final_kernel(glob, me, held, shared, in_k, in_v, out_k, out_v, summed, sems):
    del in_k, in_v
    blocks = out_k.shape[0]
    for g in range(GLOBAL):

        @pl.when(glob[g] // blocks == me[0])
        def _():
            copies = []
            for n, out in enumerate((out_k, out_v)):
                slot = 2 * g + n
                rows = shared[slot * BLOCK : (slot + 1) * BLOCK].astype(jnp.float32)
                summed[slot] = held[slot] + rows
                target = out.at[glob[g] % blocks]
                copies.append(pltpu.make_async_copy(summed.at[slot], target, sems.at[slot]))
                copies[-1].start()
            for copy in copies:
                copy.wait()


def exchange(x, axis):
    return lax.all_to_all(x, axis, split_axis=0, concat_axis=0, tiled=True)


def body(queries, key_rows, value_rows, upstream, exit_weight, labels, rand_blocks, glob_blocks):
    tokens, head_dim = queries.shape
    blocks = tokens // BLOCK
    shards = lax.axis_size("seq")
    heads = lax.axis_size("head")
    myself = lax.axis_index("seq")
    bf16 = jnp.bfloat16
    f32 = jnp.float32
    keys = (3 + RAND + GLOBAL) * BLOCK
    wide = 2 * BLOCK
    ups = [(n, n + 1) for n in range(shards - 1)]
    downs = [(n + 1, n) for n in range(shards - 1)]

    me = jnp.stack([myself, jnp.full_like(myself, shards)])
    rand = lax.dynamic_slice_in_dim(rand_blocks, myself * blocks, blocks, 0)
    mine = jnp.where(rand_blocks // blocks == myself, rand_blocks % blocks, -1)
    pick = jnp.max(jnp.max(mine, axis=1).reshape(shards, blocks), axis=1)

    q = queries.reshape(blocks, BLOCK, head_dim)
    k = key_rows.reshape(blocks, BLOCK, head_dim)
    v = value_rows.reshape(blocks, BLOCK, head_dim)
    up = upstream.reshape(blocks, BLOCK, head_dim)
    weight = exit_weight.reshape(1, head_dim)
    slot_rows = wide + CHUNK
    acc3 = (blocks, BLOCK, head_dim)

    send, first, last = call(
        pack_kernel, "pack", 2, 2,
        [((shards, slot_rows, head_dim), bf16), ((wide, head_dim), bf16), ((wide, head_dim), bf16)],
        mib=None,
    )(pick, glob_blocks, k, v)
    incoming = exchange(send, "seq")
    prev = lax.ppermute(last, "seq", ups)
    after = lax.ppermute(first, "seq", downs)
    owner = glob_blocks[myself // (shards // GLOBAL)] // blocks
    piece = lax.dynamic_slice(incoming, (owner, wide, 0), (1, CHUNK, head_dim))
    shared = exchange(jnp.broadcast_to(piece, (shards, CHUNK, head_dim)), "seq")
    shared = shared.reshape(GLOBAL * wide, head_dim)

    near = (blocks, BLOCK, (3 + RAND) * BLOCK)
    terms, out, peak, total = call(
        near_kernel, "near", 2, 6, [(near, f32), (acc3, f32), (acc3, f32), (acc3, f32)]
    )(rand, me, q, k, v, prev, after, incoming)
    full = (blocks, BLOCK, keys)
    attended, mean, probs, part = call(
        forward_kernel, "forward", 0, 7, [(acc3, bf16), (acc3, f32), (full, f32), ((heads, 1, tokens), f32)]
    )(q, shared, weight, terms, out, peak, total)
    parts = exchange(part, "head")

    grad_q, acc_k, acc_v, outgoing, to_prev, to_next = call(
        backward_kernel, "backward", 1, 13,
        [(acc3, f32), (acc3, f32), (acc3, f32), ((shards, slot_rows, head_dim), bf16),
         ((wide, head_dim), bf16), ((wide, head_dim), bf16)],
    )(
        rand, parts, labels.reshape(1, tokens), q, k, v, prev, after, incoming, shared, weight, up, mean, probs
    )
    back = exchange(outgoing, "seq")
    from_prev = lax.ppermute(to_next, "seq", ups)
    from_next = lax.ppermute(to_prev, "seq", downs)
    gsum = jnp.sum(back[:, wide:].astype(f32), axis=0, keepdims=True).astype(bf16)
    gtotal = exchange(jnp.broadcast_to(gsum, (shards, CHUNK, head_dim)), "seq")
    gtotal = gtotal.reshape(GLOBAL * wide, head_dim)

    logits = jnp.sum(parts, axis=(0, 1))
    token_loss = jax.nn.softplus(logits) - labels.astype(f32) * logits

    anywhere = pl.BlockSpec(memory_space=pl.ANY)
    held3 = (2 * GLOBAL, BLOCK, head_dim)
    out_k, out_v, held = call(
        gather_kernel, "gather", 2, 5, [(acc3, f32), (acc3, f32), (held3, f32)]
    )(pick, glob_blocks, acc_k, acc_v, back, from_prev, from_next)
    out_k, out_v = pl.pallas_call(
        final_kernel,
        name="final",
        in_specs=smem(2) + vmem(2) + [anywhere] * 2,
        out_specs=(anywhere,) * 2,
        out_shape=(jax.ShapeDtypeStruct(acc3, f32),) * 2,
        scratch_shapes=[pltpu.VMEM(held3, f32), pltpu.SemaphoreType.DMA((2 * GLOBAL,))],
        input_output_aliases={4: 0, 5: 1},
        compiler_params=pltpu.CompilerParams(vmem_limit_bytes=4 * 1024 * 1024),
    )(glob_blocks, me, held, gtotal, out_k, out_v)
    flat = (tokens, head_dim)
    return (
        attended.reshape(flat),
        token_loss,
        grad_q.reshape(flat),
        out_k.reshape(flat),
        out_v.reshape(flat),
    )


def solution(mesh):
    placed = (
        P("seq", "head"),
        P("seq", "head"),
        P("seq", "head"),
        P("seq", "head"),
        P("head"),
        P("seq"),
        P(),
        P(),
    )
    return jax.shard_map(
        body,
        mesh=mesh,
        in_specs=placed,
        out_specs=(
            P("seq", "head"),
            P("seq"),
            P("seq", "head"),
            P("seq", "head"),
            P("seq", "head"),
        ),
        check_vma=False,
    )
```

```python
import math

import jax
import jax.numpy as jnp
from jax import lax
from jax.experimental import pallas as pl
from jax.experimental.pallas import tpu as pltpu
from jax.sharding import PartitionSpec as P

BLOCK = 64
RAND = 3
GLOBAL = 2
CHUNK = 8

NT = (((1,), (1,)), ((), ()))
NN = (((1,), (0,)), ((), ()))
TN = (((0,), (0,)), ((), ()))


def mm(a, b, dims):
    return lax.dot_general(a, b, dims, preferred_element_type=jnp.float32)


def smem(count):
    return [pl.BlockSpec(memory_space=pltpu.SMEM) for _ in range(count)]


def vmem(count):
    return [pl.BlockSpec(memory_space=pltpu.VMEM) for _ in range(count)]


def call(kernel, name, n_smem, n_vmem, outs, mib=40, **kw):
    if mib:
        kw["compiler_params"] = pltpu.CompilerParams(vmem_limit_bytes=mib * 1024 * 1024)
    return pl.pallas_call(
        kernel,
        name=name,
        in_specs=smem(n_smem) + vmem(n_vmem),
        out_specs=tuple(vmem(len(outs))),
        out_shape=tuple(jax.ShapeDtypeStruct(s, d) for s, d in outs),
        **kw,
    )


def pack_kernel(pick, glob, k, v, send, first, last):
    blocks = k.shape[0]
    wide = 2 * BLOCK
    per_block = BLOCK // CHUNK
    for r in range(send.shape[0]):
        at = jnp.maximum(pick[r], 0)
        send[r, :BLOCK] = k[at]
        send[r, BLOCK:wide] = v[at]
    for g in range(GLOBAL):
        at = glob[g] % blocks
        for n, src in enumerate((k, v)):
            rows = src[at].reshape(per_block, CHUNK, src.shape[2])
            lo = (2 * g + n) * per_block
            send[lo : lo + per_block, wide:] = rows
    first[:BLOCK] = k[0]
    first[BLOCK:] = v[0]
    last[:BLOCK] = k[blocks - 1]
    last[BLOCK:] = v[blocks - 1]


def near_slots(i, base, local, prev, after, incoming, rand, blocks, tail=()):
    parts = [
        local[i - 1] if i > 0 else prev[base : base + BLOCK],
        local[i],
        local[i + 1] if i < blocks - 1 else after[base : base + BLOCK],
    ]
    for j in range(RAND):
        parts.append(incoming[rand[i, j] // blocks, base : base + BLOCK])
    return jnp.concatenate(parts + list(tail), axis=0)


def global_slots(base, shared):
    lows = [g * 2 * BLOCK + base for g in range(GLOBAL)]
    return jnp.concatenate([shared[lo : lo + BLOCK] for lo in lows], axis=0)


def near_kernel(rand, me, q, k, v, prev, after, incoming, terms, out, peak, total):
    blocks = k.shape[0]
    head_dim = k.shape[2]
    keys = (3 + RAND) * BLOCK
    inv_sqrt = 1.0 / math.sqrt(head_dim)
    lane = lax.broadcasted_iota(jnp.int32, (BLOCK, keys), 1)
    for i in range(blocks):
        kk = near_slots(i, 0, k, prev, after, incoming, rand, blocks)
        vv = near_slots(i, BLOCK, v, prev, after, incoming, rand, blocks)
        s = mm(q[i], kk, NT) * inv_sqrt
        if i == 0:
            s = jnp.where((lane < BLOCK) & (me[0] == 0), -jnp.inf, s)
        if i == blocks - 1:
            void = (lane >= 2 * BLOCK) & (lane < 3 * BLOCK)
            s = jnp.where(void & (me[0] == me[1] - 1), -jnp.inf, s)
        m = jnp.max(s, axis=1, keepdims=True)
        e = jnp.exp(s - m)
        terms[i] = e
        out[i] = mm(e.astype(jnp.bfloat16), vv, NN)
        peak[i] = jnp.broadcast_to(m, (BLOCK, head_dim))
        total[i] = jnp.broadcast_to(jnp.sum(e, axis=1, keepdims=True), (BLOCK, head_dim))


def forward_kernel(q, shared, weight, terms, out, peak, total, attended, mean, probs, part):
    blocks, _, head_dim = q.shape
    flat = (blocks * BLOCK, head_dim)
    inv_sqrt = 1.0 / math.sqrt(head_dim)
    w8 = jnp.broadcast_to(weight[...], (8, head_dim))
    s = mm(q[...].reshape(flat), global_slots(0, shared), NT) * inv_sqrt
    old = peak[...].reshape(flat)
    m = jnp.maximum(old, jnp.max(s, axis=1, keepdims=True))
    e = jnp.exp(s - m)
    shift = jnp.exp(old - m)
    inv = 1.0 / (shift * total[...].reshape(flat) + jnp.sum(e, axis=1, keepdims=True))
    scale = (shift * inv).reshape(blocks, BLOCK, head_dim)
    near = (3 + RAND) * BLOCK
    for lo in range(0, near, head_dim):
        probs[:, :, lo : lo + head_dim] = terms[:, :, lo : lo + head_dim] * scale
    probs[:, :, near:] = (e * inv).reshape(blocks, BLOCK, head_dim)
    a = out[...].reshape(flat) * shift + mm(e.astype(jnp.bfloat16), global_slots(BLOCK, shared), NN)
    a = a * inv
    mean[...] = a.reshape(blocks, BLOCK, head_dim)
    a = a.astype(jnp.bfloat16)
    attended[...] = a.reshape(blocks, BLOCK, head_dim)
    row = mm(w8, a, NT)[:1]
    row = jnp.concatenate(
        [row[:, lo : lo + head_dim] for lo in range(0, row.shape[1], head_dim)], axis=0
    )
    for r in range(part.shape[0]):
        part[r] = row


def backward_kernel(
    rand, parts, labels, q, k, v, prev, after, incoming, shared, weight, upstream, mean, probs,
    grad_q, acc_k, acc_v, outgoing, to_prev, to_next,
):
    blocks = k.shape[0]
    head_dim = k.shape[2]
    inv_sqrt = 1.0 / math.sqrt(head_dim)
    bf16 = jnp.bfloat16
    logits = jnp.sum(parts[...], axis=0)
    logits = jnp.concatenate([logits[n : n + 1] for n in range(logits.shape[0])], axis=1)
    slope = lax.logistic(logits) - labels[...].astype(jnp.float32)
    column = jnp.transpose(jnp.broadcast_to(slope, (8, slope.shape[1])))[:, :1]
    w = weight[...].astype(jnp.float32)
    gk = global_slots(0, shared)
    gv = global_slots(BLOCK, shared)
    glob_k = jnp.zeros((GLOBAL * BLOCK, head_dim), jnp.float32)
    glob_v = jnp.zeros((GLOBAL * BLOCK, head_dim), jnp.float32)
    none = jnp.zeros((BLOCK, head_dim), bf16)
    own = []
    for i in range(blocks):
        kk = near_slots(i, 0, k, prev, after, incoming, rand, blocks, [gk])
        d = column[i * BLOCK : (i + 1) * BLOCK]
        g = (upstream[i].astype(jnp.float32) + d * w).astype(bf16)
        vv = near_slots(i, BLOCK, v, prev, after, incoming, rand, blocks, [gv])
        p = probs[i]
        dp = mm(g, vv, NT)
        dot = jnp.sum(g.astype(jnp.float32) * mean[i], axis=1, keepdims=True)
        ds = (p * (dp - dot) * inv_sqrt).astype(bf16)
        grad_q[i] = mm(ds, kk, NN)
        left = jnp.concatenate([ds, p.astype(bf16)], axis=0)
        right = jnp.concatenate(
            [jnp.concatenate([q[i], none], axis=1), jnp.concatenate([none, g], axis=1)], axis=0
        )
        both = mm(left, right, TN)
        dk = both[:, :head_dim]
        dv = both[:, head_dim:]
        for j in range(RAND):
            lo = (3 + j) * BLOCK
            at = rand[i, j] // blocks
            outgoing[at, :BLOCK] = dk[lo : lo + BLOCK].astype(bf16)
            outgoing[at, BLOCK : 2 * BLOCK] = dv[lo : lo + BLOCK].astype(bf16)
        glob_k = glob_k + dk[(3 + RAND) * BLOCK :]
        glob_v = glob_v + dv[(3 + RAND) * BLOCK :]
        own.append((dk[: 3 * BLOCK], dv[: 3 * BLOCK]))
    for which, acc in enumerate((acc_k, acc_v)):
        lo = which * BLOCK
        for i in range(blocks):
            total = own[i][which][BLOCK : 2 * BLOCK]
            if i < blocks - 1:
                total = total + own[i + 1][which][:BLOCK].astype(bf16).astype(jnp.float32)
            if i > 0:
                total = total + own[i - 1][which][2 * BLOCK :].astype(bf16).astype(jnp.float32)
            acc[i] = total
        to_prev[lo : lo + BLOCK] = own[0][which][:BLOCK].astype(bf16)
        to_next[lo : lo + BLOCK] = own[blocks - 1][which][2 * BLOCK :].astype(bf16)
    per_block = BLOCK // CHUNK
    for n in range(2 * GLOBAL):
        lo = (n // 2) * BLOCK
        rows = (glob_v if n % 2 else glob_k)[lo : lo + BLOCK].astype(bf16)
        outgoing[n * per_block : (n + 1) * per_block, 2 * BLOCK :] = rows.reshape(per_block, CHUNK, head_dim)


def gather_kernel(pick, glob, acc_k, acc_v, back, from_prev, from_next, out_k, out_v, held):
    blocks = acc_k.shape[0]
    f32 = jnp.float32
    out_k[...] = acc_k[...]
    out_v[...] = acc_v[...]
    out_k[0] = out_k[0] + from_prev[:BLOCK].astype(f32)
    out_v[0] = out_v[0] + from_prev[BLOCK:].astype(f32)
    out_k[blocks - 1] = out_k[blocks - 1] + from_next[:BLOCK].astype(f32)
    out_v[blocks - 1] = out_v[blocks - 1] + from_next[BLOCK:].astype(f32)
    for r in range(back.shape[0]):
        at = pick[r]

        @pl.when(at >= 0)
        def _():
            out_k[at] = out_k[at] + back[r, :BLOCK].astype(f32)
            out_v[at] = out_v[at] + back[r, BLOCK : 2 * BLOCK].astype(f32)

    for g in range(GLOBAL):
        at = glob[g] % blocks
        held[2 * g] = out_k[at]
        held[2 * g + 1] = out_v[at]


def final_kernel(glob, me, held, shared, in_k, in_v, out_k, out_v, summed, sems):
    del in_k, in_v
    blocks = out_k.shape[0]
    for g in range(GLOBAL):

        @pl.when(glob[g] // blocks == me[0])
        def _():
            copies = []
            for n, out in enumerate((out_k, out_v)):
                slot = 2 * g + n
                rows = shared[slot * BLOCK : (slot + 1) * BLOCK].astype(jnp.float32)
                summed[slot] = held[slot] + rows
                target = out.at[glob[g] % blocks]
                copies.append(pltpu.make_async_copy(summed.at[slot], target, sems.at[slot]))
                copies[-1].start()
            for copy in copies:
                copy.wait()


def exchange(x, axis):
    return lax.all_to_all(x, axis, split_axis=0, concat_axis=0, tiled=True)


def body(queries, key_rows, value_rows, upstream, exit_weight, labels, rand_blocks, glob_blocks):
    tokens, head_dim = queries.shape
    blocks = tokens // BLOCK
    shards = lax.axis_size("seq")
    heads = lax.axis_size("head")
    myself = lax.axis_index("seq")
    bf16 = jnp.bfloat16
    f32 = jnp.float32
    keys = (3 + RAND + GLOBAL) * BLOCK
    wide = 2 * BLOCK
    ups = [(n, n + 1) for n in range(shards - 1)]
    downs = [(n + 1, n) for n in range(shards - 1)]

    me = jnp.stack([myself, jnp.full_like(myself, shards)])
    rand = lax.dynamic_slice_in_dim(rand_blocks, myself * blocks, blocks, 0)
    mine = jnp.where(rand_blocks // blocks == myself, rand_blocks % blocks, -1)
    pick = jnp.max(jnp.max(mine, axis=1).reshape(shards, blocks), axis=1)

    q = queries.reshape(blocks, BLOCK, head_dim)
    k = key_rows.reshape(blocks, BLOCK, head_dim)
    v = value_rows.reshape(blocks, BLOCK, head_dim)
    up = upstream.reshape(blocks, BLOCK, head_dim)
    weight = exit_weight.reshape(1, head_dim)
    slot_rows = wide + CHUNK
    acc3 = (blocks, BLOCK, head_dim)

    send, first, last = call(
        pack_kernel, "pack", 2, 2,
        [((shards, slot_rows, head_dim), bf16), ((wide, head_dim), bf16), ((wide, head_dim), bf16)],
        mib=None,
    )(pick, glob_blocks, k, v)
    incoming = exchange(send, "seq")
    prev = lax.ppermute(last, "seq", ups)
    after = lax.ppermute(first, "seq", downs)
    owner = glob_blocks[myself // (shards // GLOBAL)] // blocks
    piece = lax.dynamic_slice(incoming, (owner, wide, 0), (1, CHUNK, head_dim))
    shared = exchange(jnp.broadcast_to(piece, (shards, CHUNK, head_dim)), "seq")
    shared = shared.reshape(GLOBAL * wide, head_dim)

    near = (blocks, BLOCK, (3 + RAND) * BLOCK)
    terms, out, peak, total = call(
        near_kernel, "near", 2, 6, [(near, f32), (acc3, f32), (acc3, f32), (acc3, f32)]
    )(rand, me, q, k, v, prev, after, incoming)
    full = (blocks, BLOCK, keys)
    attended, mean, probs, part = call(
        forward_kernel, "forward", 0, 7, [(acc3, bf16), (acc3, f32), (full, f32), ((heads, tokens // head_dim, head_dim), f32)]
    )(q, shared, weight, terms, out, peak, total)
    parts = exchange(part, "head")

    grad_q, acc_k, acc_v, outgoing, to_prev, to_next = call(
        backward_kernel, "backward", 1, 13,
        [(acc3, f32), (acc3, f32), (acc3, f32), ((shards, slot_rows, head_dim), bf16),
         ((wide, head_dim), bf16), ((wide, head_dim), bf16)],
    )(
        rand, parts, labels.reshape(1, tokens), q, k, v, prev, after, incoming, shared, weight, up, mean, probs
    )
    back = exchange(outgoing, "seq")
    from_prev = lax.ppermute(to_next, "seq", ups)
    from_next = lax.ppermute(to_prev, "seq", downs)
    gsum = jnp.sum(back[:, wide:].astype(f32), axis=0, keepdims=True).astype(bf16)
    gtotal = exchange(jnp.broadcast_to(gsum, (shards, CHUNK, head_dim)), "seq")
    gtotal = gtotal.reshape(GLOBAL * wide, head_dim)

    logits = jnp.sum(parts, axis=0).reshape(tokens)
    token_loss = jax.nn.softplus(logits) - labels.astype(f32) * logits

    anywhere = pl.BlockSpec(memory_space=pl.ANY)
    held3 = (2 * GLOBAL, BLOCK, head_dim)
    out_k, out_v, held = call(
        gather_kernel, "gather", 2, 5, [(acc3, f32), (acc3, f32), (held3, f32)]
    )(pick, glob_blocks, acc_k, acc_v, back, from_prev, from_next)
    out_k, out_v = pl.pallas_call(
        final_kernel,
        name="final",
        in_specs=smem(2) + vmem(2) + [anywhere] * 2,
        out_specs=(anywhere,) * 2,
        out_shape=(jax.ShapeDtypeStruct(acc3, f32),) * 2,
        scratch_shapes=[pltpu.VMEM(held3, f32), pltpu.SemaphoreType.DMA((2 * GLOBAL,))],
        input_output_aliases={4: 0, 5: 1},
        compiler_params=pltpu.CompilerParams(vmem_limit_bytes=4 * 1024 * 1024),
    )(glob_blocks, me, held, gtotal, out_k, out_v)
    flat = (tokens, head_dim)
    return (
        attended.reshape(flat),
        token_loss,
        grad_q.reshape(flat),
        out_k.reshape(flat),
        out_v.reshape(flat),
    )


def solution(mesh):
    placed = (
        P("seq", "head"),
        P("seq", "head"),
        P("seq", "head"),
        P("seq", "head"),
        P("head"),
        P("seq"),
        P(),
        P(),
    )
    return jax.shard_map(
        body,
        mesh=mesh,
        in_specs=placed,
        out_specs=(
            P("seq", "head"),
            P("seq"),
            P("seq", "head"),
            P("seq", "head"),
            P("seq", "head"),
        ),
        check_vma=False,
    )
```
